128 devices in a mesh: dev: 128 (over x, z, y, core).
Axes of the slice: x: 4, y: 4, z: 4, core: 2. Of those that a mesh axis runs over, the one named last changes fastest.
Arguments:
- node_coords: float32 [3, 65536], P(None, 'dev'), may hold values from 0 to 1
- node_disp: float32 [3, 65536], P(None, 'dev'), may hold values from -6 to 6
- node_list: int32 [128, 1024], P('dev'), may hold values from 0 to 65535, as said below
- factor: float32 [128, 1024, 1024], P('dev'), may hold values from -1 to 2, as said below
- fluid_coords: float32 [3, 524288], P(None, 'dev'), may hold values from 0 to 1
- fluid_loads: float32 [3, 524288], P(None, 'dev'), may hold values from -6 to 6
- fluid_patch: int32 [524288, 4], P('dev'), may hold values from 0 to 127, all different within a row; in each aligned block of 4096 rows (0 to 4095, 4096 to 8191, ...) at most 256 rows name the same one
- blend_raw: float32 [524288, 4], P('dev'), may hold values from 0.1 to 1
Outputs:
- fluid_disp: float32 [3, 524288], P(None, 'dev')
- node_loads: float32 [3, 65536], P(None, 'dev')
The draws below stay inside these ranges and needn't reach their ends.
Inputs may be any that keep to these rules, and one draw needn't show every extreme that they name: `node_list`: the 1024 entries of one patch name nodes of exactly 64 distinct devices (node n belongs to device n // 512), exactly 16 entries for each of them; a node may appear more than once. factor[p] is lower triangular with diagonal entries between 1 and 2. `fluid_patch`: in each aligned block of 4096 points no patch is named by more than 256 points.
All inputs are finite; a program needn't handle non-finite values.
Results may differ from the reference program's by a relative error of at most 0.0003.
Values sent between devices are 32-bit elements; how exact they have to be, the bound alone decides.
A program may use at most 192 MiB of HBM per device.

```python
import math
import jax
import jax.numpy as jnp
import numpy as np
from jax import lax

PN = 1024
SLOTS = 4
FLUID_DEV = 4096
PATCHES = 128
NODE_DEV = 512
NODES = 65536
FLUID = 524288
MOST = 256
CAP = 16
OWNERS = 64


def draw_node_list(key, part):

    def one_device(dev_key):
        first, second, third = jax.random.split(dev_key, 3)
        chosen = jax.random.permutation(first, PATCHES)[:OWNERS]
        owning = chosen[jnp.arange(PN) // CAP]
        local_ids = jax.random.randint(second, (PN,), 0, NODE_DEV)
        node_ids = owning * NODE_DEV + local_ids
        return jax.random.permutation(third, node_ids)
    dev_keys = jax.vmap(lambda index: jax.random.fold_in(key, index))(jnp.arange(PATCHES))
    return jax.vmap(one_device)(dev_keys).astype(jnp.int32)


def draw_factor(key, part):
    first, second = jax.random.split(jax.random.fold_in(key, 17))
    rows_idx = jnp.arange(PN)[:, None]
    cols_idx = jnp.arange(PN)[None, :]
    lower = jax.random.normal(first, (PATCHES, PN, PN), jnp.float32) * (0.8 / math.sqrt(PN))
    diagonal = jax.random.uniform(second, (PATCHES, PN, 1), jnp.float32, 1.0, 2.0)
    result = jnp.where(cols_idx < rows_idx, lower, 0.0) + jnp.where(cols_idx == rows_idx, diagonal, 0.0)
    return result.astype(jnp.float32)


def levels(rng, dims, cuts, low, high):
    factor_of, own = 1.0, jax.random.fold_in(rng, 6)
    for axis_at, blocks in cuts:
        steps = jnp.exp(jax.random.uniform(jax.random.fold_in(own, axis_at), (blocks,), jnp.float32, low / len(cuts), high / len(cuts)))
        factor_of = factor_of * jnp.repeat(steps, dims[axis_at] // blocks).reshape([-1 if axis == axis_at else 1 for axis in range(len(dims))])
    return factor_of


def assign_block(key, own, number, rows, number_of, top, limit, slope):
    ranking = jax.random.permutation(key, number_of)
    crowded, usual = portions_of(number_of, rows * top, limit, slope, True), portions_of(number_of, rows * top, limit, slope, False)
    places = jnp.arange(number_of)

    def named(lengths, turn):
        used = int((lengths > 0).sum())
        fixed = max(1, used // 4)
        passed = fixed + (places - fixed + turn * (used - fixed)) % max(1, number_of - fixed)
        return jnp.zeros((number_of,), jnp.int32).at[ranking[jnp.where(places < fixed, places, passed)]].set(jnp.asarray(lengths, jnp.int32))

    lengths = jnp.where(number % 4 == 0, named(crowded, number // 4), named(usual, number - number // 4 - 1))
    mixed = jax.random.permutation(jax.random.fold_in(own, 3), number_of)
    donor, taker = mixed[0:number_of // 2 * 2:2], mixed[1:number_of // 2 * 2:2]
    slack = jnp.minimum(lengths[donor] - 1, limit - lengths[taker]) // 2
    slack = jnp.where((donor == ranking[0]) | (taker == ranking[0]) | (lengths[taker] == 0), 0, jnp.maximum(slack, 0))
    passed = jax.random.randint(jax.random.fold_in(own, 4), (number_of // 2,), 0, 1 << 20) % (slack + 1)
    lengths = lengths.at[donor].add(-passed).at[taker].add(passed)
    labels = jnp.searchsorted(jnp.cumsum(lengths), jnp.arange(rows * top), side="right").astype(jnp.int32)
    grid = labels.reshape(top, rows).T
    grid = grid[jax.random.permutation(jax.random.fold_in(own, 1), rows)]
    turn = jax.random.randint(jax.random.fold_in(own, 2), (rows, 1), 0, top)
    return jnp.take_along_axis(grid, (jnp.arange(top)[None, :] + turn) % top, axis=1)


def portions_of(count, total, limit, slope, full):
    weights = [(1 << 20) // math.isqrt(rank ** slope) + 1 for rank in range(1, count + 1)]
    largest = limit if full else min(limit, max(-(-total // count), total * weights[0] // sum(weights)))
    least = 1 if total - largest >= count - 1 else 0
    given, surplus = [largest] + [least] * (count - 1), total - largest - least * (count - 1)
    while surplus > 0:
        candidates = [i for i in range(1, count) if given[i] < largest] or [i for i in range(1, count) if given[i] < limit]
        pool, budget = sum([weights[i] for i in candidates]), surplus
        for i in candidates:
            addition = min(limit - given[i], max(1, budget * weights[i] // pool), surplus)
            given[i] = given[i] + addition
            surplus = surplus - addition
    return np.array(given)


def normal_values(key, shape, deviation, reach, shards=(), kind=jnp.bfloat16):
    values = deviation * jax.random.normal(key, shape, jnp.float32)
    if shards:
        values = values * levels(key, shape, shards, -0.22, 0.18)
    return jnp.clip(values, -reach, reach).astype(kind)


def setup_inputs(seed: int = 0) -> dict:
    splits = jax.random.split(jax.random.key(seed), 9)
    node_coords = jnp.clip(1.0 * jax.random.uniform(splits[0], (3, NODES), jnp.float32) ** levels(splits[0], (3, NODES), ((1, 128),), -0.2, 0.2), 0.0, 1.0)
    node_disp = normal_values(splits[1], (3, NODES), 1.0, 6.0, ((1, 128),), jnp.float32)
    node_list = draw_node_list(jax.random.fold_in(splits[8], 71), 0)
    factor = draw_factor(jax.random.fold_in(splits[8], 71), 0)
    fluid_coords = jnp.clip(1.0 * jax.random.uniform(splits[4], (3, FLUID), jnp.float32) ** levels(splits[4], (3, FLUID), ((1, 128),), -0.2, 0.2), 0.0, 1.0)
    fluid_loads = normal_values(splits[5], (3, FLUID), 1.0, 6.0, ((1, 128),), jnp.float32)
    fluid_patch_keys = jax.random.split(jax.random.fold_in(splits[6], 1), FLUID // FLUID_DEV)
    fluid_patch_turns = jax.random.permutation(jax.random.fold_in(splits[6], 3), FLUID // FLUID_DEV)
    fluid_patch = jax.vmap(lambda own, number: assign_block(jax.random.fold_in(splits[6], 2), own, number, FLUID_DEV, PATCHES, SLOTS, MOST, 1))(fluid_patch_keys, fluid_patch_turns).reshape((FLUID, SLOTS))
    blend_raw = jnp.clip(jnp.exp(math.log(1.0) - 2.3025851 * jax.random.uniform(splits[7], (FLUID, SLOTS), jnp.float32) ** levels(splits[7], (FLUID, SLOTS), ((0, 128),), -0.2, 0.2)), 0.1, 1.0)
    return {"node_coords": node_coords, "node_disp": node_disp, "node_list": node_list, "factor": factor, "fluid_coords": fluid_coords, "fluid_loads": fluid_loads, "fluid_patch": fluid_patch, "blend_raw": blend_raw}


kernel_gain = 8.0
highest = lax.Precision.HIGHEST

def kernel_tile(points, centres):
    squared = jnp.zeros((points.shape[1], centres.shape[1]), jnp.float32)
    for component in range(3):
        offset = points[component][:, None] - centres[component][None, :]
        squared = squared + offset * offset
    return lax.rsqrt(1.0 + kernel_gain * squared) / math.sqrt(PN)

def apply_inverse(values, inverse):
    partial_value = lax.dot_general(values, inverse, (((1,), (1,)), ((), ())), precision=highest)
    return jnp.dot(partial_value, inverse, precision=highest)

def rank_in_block(targets, classes):
    onehot = (targets[:, None] == jnp.arange(classes, dtype=jnp.int32)[None, :]).astype(jnp.int32)
    before = jnp.cumsum(onehot, axis=0) - onehot
    return lax.optimization_barrier(jnp.sum(before * onehot, axis=1)).astype(jnp.int32)

def reference(node_coords, node_disp, node_list, factor, fluid_coords, fluid_loads, fluid_patch, blend_raw):
    devices = PATCHES
    blends = blend_raw / lax.optimization_barrier(jnp.sum(blend_raw, axis=1, keepdims=True))
    weight_flat = blends.reshape(-1)
    targets = fluid_patch.reshape(devices, FLUID_DEV * SLOTS)
    placed = lax.map(lambda target: rank_in_block(target, devices), targets)
    columns = jnp.arange(devices, dtype=jnp.int32)[:, None] * MOST + placed
    entries = jnp.arange(FLUID * SLOTS, dtype=jnp.int32)
    slot_table = jnp.full((devices, devices * MOST), -1, jnp.int32)
    slot_table = slot_table.at[targets.reshape(-1), columns.reshape(-1)].set(entries)

    def one_patch(packed):
        node_ids, inverse, bucket_rows = packed
        centres = node_coords[:, node_ids]
        coeffs = apply_inverse(node_disp[:, node_ids], inverse)
        is_live = bucket_rows >= 0
        safe_rows = jnp.where(is_live, bucket_rows, 0)
        point_row = safe_rows // SLOTS
        weighted = jnp.where(is_live[None, :], weight_flat[safe_rows][None, :] * fluid_loads[:, point_row], 0.0)
        tile_vals = kernel_tile(fluid_coords[:, point_row], centres)
        value = lax.dot_general(coeffs, tile_vals, (((1,), (1,)), ((), ())), precision=highest)
        accumulated = lax.dot_general(weighted, tile_vals, (((1,), (0,)), ((), ())), precision=highest)
        return (value, apply_inverse(accumulated, inverse))
    values, patch_loads = lax.map(one_patch, (node_list, factor, slot_table))
    flat_rows = slot_table.reshape(-1)
    is_live = flat_rows >= 0
    safe_rows = jnp.where(is_live, flat_rows, 0)
    flat_values = jnp.transpose(values, (1, 0, 2)).reshape(3, -1)
    per_entry = jnp.zeros((3, FLUID * SLOTS), jnp.float32).at[:, safe_rows].add(jnp.where(is_live[None, :], flat_values, 0.0))
    fluid_disp = lax.optimization_barrier(jnp.sum((per_entry * weight_flat[None, :]).reshape(3, FLUID, SLOTS), axis=2))
    flat_loads = jnp.transpose(patch_loads, (1, 0, 2)).reshape(3, -1)
    node_loads = jnp.zeros((3, NODES), jnp.float32).at[:, node_list.reshape(-1)].add(flat_loads)
    return (fluid_disp, node_loads)
```

```python
import jax
import jax.numpy as jnp
from jax import lax
from jax.experimental import pallas as pl
from jax.experimental.pallas import tpu as pltpu
from jax.sharding import PartitionSpec as P

PN = 1024
SLOTS = 4
PATCHES = 128
NODE_DEV = 512
LANES = 128
SIDE = 4
STRIDE = (32, 8, 2)
GAIN = 8.0

f32 = jnp.float32
bf16 = jnp.bfloat16
VMEM = pltpu.VMEM
MESH = pl.DeviceIdType.MESH


def place():
    me = lax.axis_index("dev")
    return me, lax.rem(me, 2), tuple(lax.rem(me // s, SIDE) for s in STRIDE)


def peer_of(me, spot, axis, step):
    return me + (lax.rem(spot[axis] + step, SIDE) - spot[axis]) * STRIDE[axis]


def meet(me, core, spot):
    barrier = pltpu.get_barrier_semaphore()
    for axis in range(3):
        for step in (1, 2, 3):
            peer = peer_of(me, spot, axis, step)
            pl.semaphore_signal(barrier, inc=1, device_id=(peer,), device_id_type=MESH)
    pl.semaphore_signal(barrier, inc=1, device_id=(me + 1 - 2 * core,), device_id_type=MESH)
    pl.semaphore_wait(barrier, 10)


def send(src, dst, send_sem, recv_sem, device):
    copy = pltpu.make_async_remote_copy(
        src_ref=src,
        dst_ref=dst,
        send_sem=send_sem,
        recv_sem=recv_sem,
        device_id=(device,),
        device_id_type=MESH,
    )
    copy.start()
    return copy


def gather_stages(out, place_now, sems):
    me, core, spot = place_now
    send_sem, recv_sem, core_send, core_recv = sems
    for stage in range(3):
        copies = []
        for g in range(3):
            axis = (g + stage) % 3
            done = [(g + t) % 3 for t in range(stage)]
            where = tuple(slice(None) if a in done else spot[a] for a in range(3)) + (core, g)
            for step in (1, 2, 3):
                part = out.at[where]
                copies.append(
                    send(
                        part,
                        part,
                        send_sem.at[stage, g, step - 1],
                        recv_sem.at[stage, g, 3 - step],
                        peer_of(me, spot, axis, step),
                    )
                )
        for copy in copies:
            copy.wait()
    part = out.at[:, :, :, core]
    send(part, part, core_send, core_recv, me + 1 - 2 * core).wait()


def sum_kernel(terms, out, core_in, s1, r2, s2, r3, s3, r4, send_sem, recv_sem, core_send, core_recv):
    me, core, spot = place()
    meet(me, core, spot)
    part = terms.at[:, :, :, 1 - core]
    send(part, core_in, core_send, core_recv, me + 1 - 2 * core).wait()
    for a in range(SIDE):
        for g in range(3):
            s1[g, a] = terms[a, :, :, core, g] + core_in[a, :, :, g]
    sums, landed = (s1, s2, s3), (r2, r3, r4)
    for stage in range(3):
        src, dst = sums[stage], landed[stage]
        ahead = []
        for g in range(3):
            gone = [(g + t) % 3 for t in range(stage)]
            ahead.append([a for a in range(3) if a not in gone].index((g + stage) % 3))
        copies = []
        for g in range(3):
            axis = (g + stage) % 3
            for step in (1, 2, 3):
                to = lax.rem(spot[axis] + step, SIDE)
                copies.append(
                    send(
                        src.at[(g,) + (slice(None),) * ahead[g] + (to,)],
                        dst.at[g, 3 - step],
                        send_sem.at[stage, g, step - 1],
                        recv_sem.at[stage, g, 3 - step],
                        peer_of(me, spot, axis, step),
                    )
                )
        for g in range(3):
            axis = (g + stage) % 3
            for k in range(3):
                copies[3 * g + k].wait_recv()
            mine = (g,) + (slice(None),) * ahead[g] + (spot[axis],)
            total = (src[mine] + dst[g, 0]) + (dst[g, 1] + dst[g, 2])
            if stage < 2:
                sums[stage + 1][g] = total
            else:
                out[g] = total
        for copy in copies:
            copy.wait_send()


def sum_scatter(terms, collective_id):
    tail = terms.shape[5:]
    dma = pltpu.SemaphoreType.DMA
    return pl.pallas_call(
        sum_kernel,
        out_shape=jax.ShapeDtypeStruct((3,) + tail, f32),
        in_specs=[pl.BlockSpec(memory_space=VMEM)],
        out_specs=pl.BlockSpec(memory_space=VMEM),
        scratch_shapes=[
            VMEM((4, 4, 4, 3) + tail, f32),
            VMEM((3, 4, 4, 4) + tail, f32),
            VMEM((3, 3, 4, 4) + tail, f32),
            VMEM((3, 4, 4) + tail, f32),
            VMEM((3, 3, 4) + tail, f32),
            VMEM((3, 4) + tail, f32),
            VMEM((3, 3) + tail, f32),
            dma((3, 3, 3)),
            dma((3, 3, 3)),
            dma,
            dma,
        ],
        compiler_params=pltpu.CompilerParams(collective_id=collective_id, has_side_effects=True),
    )(terms)


def node_kernel(coords, disp, out, *sems):
    me, core, spot = place()
    for g in range(3):
        for r in range(4):
            lanes = pl.ds(r * LANES, LANES)
            out[spot[0], spot[1], spot[2], core, g, pl.ds(r, 1), :] = coords[pl.ds(g, 1), lanes]
            out[spot[0], spot[1], spot[2], core, g, pl.ds(4 + r, 1), :] = disp[pl.ds(g, 1), lanes]
    meet(me, core, spot)
    gather_stages(out, (me, core, spot), sems)


def patch_kernel(rows, out, own_sem, *sems):
    me, core, spot = place()
    own = pltpu.make_async_copy(rows, out.at[spot[0], spot[1], spot[2], core], own_sem)
    own.start()
    meet(me, core, spot)
    own.wait()
    gather_stages(out, (me, core, spot), sems)


def gather_call(kernel, args, rows, own, collective_id):
    dma = pltpu.SemaphoreType.DMA
    return pl.pallas_call(
        kernel,
        out_shape=jax.ShapeDtypeStruct((4, 4, 4, 2, 3, rows, LANES), f32),
        in_specs=[pl.BlockSpec(memory_space=VMEM)] * len(args),
        out_specs=pl.BlockSpec(memory_space=VMEM),
        scratch_shapes=[dma] * own + [dma((3, 3, 3)), dma((3, 3, 3)), dma, dma],
        compiler_params=pltpu.CompilerParams(collective_id=collective_id, has_side_effects=True),
    )(*args)


def halves(x):
    high = x.astype(bf16)
    return high, (x - high.astype(f32)).astype(bf16)


def times_factor(values, high, low, contract):
    top, bottom = halves(values)
    both = jnp.concatenate([top, bottom], axis=0)
    dims = (((1,), (contract,)), ((), ()))
    first = lax.dot_general(both, high, dims, preferred_element_type=f32)
    second = lax.dot_general(both, low, dims, preferred_element_type=f32)
    return (first[:8] + first[8:]) + (second[:8] + second[8:])


def apply_inverse(values, high, low):
    return times_factor(times_factor(values, high, low, 1), high, low, 0)


def owners(ids):
    device = lax.shift_right_logical(ids, 9)
    local = lax.bitwise_and(ids, NODE_DEV - 1)
    at_device = lax.broadcasted_iota(jnp.int32, (PATCHES, PN), 0) == device
    at_local = lax.broadcasted_iota(jnp.int32, (NODE_DEV, PN), 0) == local
    return at_device, jnp.where(at_local, 1.0, 0.0).astype(bf16)


def coeff_kernel(table, ids, factor, out):
    at_device, at_local = owners(ids[...])
    pieces = []
    for g in range(3):
        for h in range(2):
            row = [table[pl.ds(8 * g + 4 * h + r, PATCHES, stride=24), :] for r in range(4)]
            pieces.append(jnp.concatenate(row, axis=1))
    stacked = jnp.concatenate(pieces, axis=0)
    high, low = halves(stacked)
    found = jnp.dot(high, at_local, preferred_element_type=f32)
    found = found + jnp.dot(low, at_local, preferred_element_type=f32)
    picked = []
    for c in range(6):
        mine = found[c * PATCHES : (c + 1) * PATCHES]
        picked.append(jnp.sum(jnp.where(at_device, mine, 0.0), axis=0, keepdims=True))
    moved = jnp.concatenate([picked[1], picked[3], picked[5]] + [jnp.zeros((5, PN), f32)], axis=0)
    coeffs = apply_inverse(moved, *halves(factor[...]))
    for g in range(3):
        scaled = picked[2 * g] * (-2.0 * GAIN)
        for s in range(8):
            lanes = slice(s * LANES, (s + 1) * LANES)
            out[g, pl.ds(s, 1), :] = scaled[:, lanes]
            out[g, pl.ds(8 + s, 1), :] = coeffs[g : g + 1, lanes]


def load_kernel(summed, ids, factor, out):
    rows = jnp.concatenate([summed[:, s, :] for s in range(8)], axis=1)
    rows = jnp.concatenate([rows, jnp.zeros((5, PN), f32)], axis=0)
    loads = apply_inverse(rows * (1.0 / 32.0), *halves(factor[...]))
    at_device, at_local = owners(ids[...])
    parts = []
    for g in range(3):
        parts.extend(halves(jnp.where(at_device, loads[g : g + 1], 0.0)))
    terms = lax.dot_general(
        jnp.concatenate(parts, axis=0),
        at_local,
        (((1,), (1,)), ((), ())),
        preferred_element_type=f32,
    )
    for g in range(3):
        base = 2 * g * PATCHES
        term = terms[base : base + PATCHES] + terms[base + PATCHES : base + 2 * PATCHES]
        for r in range(4):
            lanes = slice(r * LANES, (r + 1) * LANES)
            out[pl.ds(4 * g + r, PATCHES, stride=12), :] = term[:, lanes]


def in_vmem(kernel, args, shape):
    return pl.pallas_call(
        kernel,
        out_shape=jax.ShapeDtypeStruct(shape, f32),
        in_specs=[pl.BlockSpec(memory_space=VMEM)] * len(args),
        out_specs=pl.BlockSpec(memory_space=VMEM),
        compiler_params=pltpu.CompilerParams(vmem_limit_bytes=56 * 2**20),
    )(*args)


def fold_rows(regs, masks):
    for shift, mask in zip((4, 2, 1), masks):
        n = len(regs) // 2
        out = []
        for a, b in zip(regs[:n], regs[n:]):
            if shift == 4:
                out.append(jnp.where(mask, a, b) + pltpu.roll(jnp.where(mask, b, a), 4, 0))
            else:
                left, right = pltpu.roll(a, 8 - shift, 0), pltpu.roll(b, shift, 0)
                out.append(jnp.where(mask, a, b) + jnp.where(mask, left, right))
        regs = out
    return regs[0]


FIELDS = 11


def fluid_kernel(patch, coords, loads, blend, table, disp, acc, norm, record, wide, sums):
    points = coords.shape[1]
    acc[...] = jnp.zeros_like(acc)
    row = lax.broadcasted_iota(jnp.int32, (8, LANES), 0)
    masks = [(row & bit) == 0 for bit in (4, 2, 1)]

    def patch_step(p, _):
        y = [table[6 * p + 2 * c] for c in range(3)]
        total = (y[0] * y[0] + y[1] * y[1]) + y[2] * y[2]
        norm[p] = 1.0 + total * (1.0 / (4.0 * GAIN))
        return 0

    lax.fori_loop(0, PATCHES, patch_step, 0)

    def record_step(j, _):
        lanes = pl.ds(pl.multiple_of(j * LANES, LANES), LANES)
        x, b = coords[:, lanes], blend[:, lanes]
        square = GAIN * jnp.sum(x * x, axis=0, keepdims=True)
        share = b / jnp.sum(b, axis=0, keepdims=True)
        field = jnp.concatenate([x, loads[:, lanes], square, share, jnp.zeros((5, LANES), f32)], axis=0)
        record[lanes, pl.ds(0, 16)] = field.T
        return 0

    lax.fori_loop(0, points // LANES, record_step, 0)

    def spread(group, slot):
        block = record[pl.ds(pl.multiple_of(group * 8, 8), 8), :]
        for j in range(FIELDS):
            wide[slot * FIELDS + j] = jnp.broadcast_to(block[:, j : j + 1], (8, LANES))

    groups = points // 8
    spread(0, 0)

    def point_step(group, _):
        first = pl.multiple_of(group * 8, 8)
        slot = lax.rem(group, 2)
        spread(jnp.minimum(group + 1, groups - 1), 1 - slot)
        names = [patch.at[s, pl.ds(first, 8)] for s in range(SLOTS)]
        value = [[], [], []]
        for q in range(8):

            def field(j):
                return wide[slot * FIELDS + j, pl.ds(q, 8, stride=0), :]

            x, y, z, square = field(0), field(1), field(2), field(6)
            force = [field(3 + c) for c in range(3)]
            ps = [names[s][q] for s in range(SLOTS)]
            term = []
            for s in range(SLOTS):
                p = ps[s]
                near = (table[6 * p] * x + table[6 * p + 2] * y) + (
                    table[6 * p + 4] * z + (norm[p] + square)
                )
                term.append(lax.rsqrt(near) * field(7 + s))
            old = [[acc[3 * p + c] for c in range(3)] for p in ps]
            for c in range(3):
                dots = [table[6 * ps[s] + 2 * c + 1] * term[s] for s in range(SLOTS)]
                value[c].append((dots[0] + dots[1]) + (dots[2] + dots[3]))
            for s in range(SLOTS):
                for c in range(3):
                    acc[3 * ps[s] + c] = old[s][c] + term[s] * force[c]
        for c in range(3):
            sums[c, pl.ds(first, 8), :] = fold_rows(value[c], masks)
        return 0

    lax.fori_loop(0, groups, point_step, 0)

    def out_step(j, _):
        lanes = pl.ds(pl.multiple_of(j * LANES, LANES), LANES)
        for c in range(3):
            disp[pl.ds(c, 1), lanes] = jnp.sum(sums[c, lanes, :].T, axis=0, keepdims=True) * (1.0 / 32.0)
        return 0

    lax.fori_loop(0, points // LANES, out_step, 0)


def fluid(patch, coords, loads, blend, table):
    points = coords.shape[1]
    return pl.pallas_call(
        fluid_kernel,
        out_shape=(
            jax.ShapeDtypeStruct((3, points), f32),
            jax.ShapeDtypeStruct((PATCHES * 3, 8, LANES), f32),
        ),
        in_specs=[pl.BlockSpec(memory_space=pltpu.SMEM)] + [pl.BlockSpec(memory_space=VMEM)] * 4,
        out_specs=[pl.BlockSpec(memory_space=VMEM)] * 2,
        scratch_shapes=[
            VMEM((PATCHES, 8, LANES), f32),
            VMEM((points, LANES), f32),
            VMEM((2 * FIELDS, 8, LANES), f32),
            VMEM((3, points, LANES), f32),
        ],
    )(patch, coords, loads, blend, table)


def local(node_coords, node_disp, node_list, factor, fluid_coords, fluid_loads, fluid_patch, blend_raw):
    inverse = factor[0]
    nodes = gather_call(node_kernel, (node_coords, node_disp), 8, 0, 0)
    nodes = nodes.reshape(PATCHES * 24, LANES)
    rows = in_vmem(coeff_kernel, (nodes, node_list, inverse), (3, 16, LANES))
    table = gather_call(patch_kernel, (rows,), 16, 1, 1)
    table = table.reshape(PATCHES * 6, 8, LANES)
    fluid_disp, terms = fluid(fluid_patch.T, fluid_coords, fluid_loads, blend_raw.T, table)
    summed = sum_scatter(terms.reshape(4, 4, 4, 2, 3, 8, LANES), 2)
    spread = in_vmem(load_kernel, (summed, node_list, inverse), (PATCHES * 12, LANES))
    owned = sum_scatter(spread.reshape(4, 4, 4, 2, 3, 4, LANES), 3)
    return fluid_disp, owned.reshape(3, NODE_DEV)


def solution(mesh):
    placed = (
        P(None, "dev"),
        P(None, "dev"),
        P("dev", None),
        P("dev", None, None),
        P(None, "dev"),
        P(None, "dev"),
        P("dev", None),
        P("dev", None),
    )
    return jax.shard_map(
        local,
        mesh=mesh,
        in_specs=placed,
        out_specs=(P(None, "dev"), P(None, "dev")),
        check_vma=False,
    )
```

```python
import jax
import jax.numpy as jnp
from jax import lax
from jax.experimental import pallas as pl
from jax.experimental.pallas import tpu as pltpu
from jax.sharding import PartitionSpec as P

PN = 1024
SLOTS = 4
PATCHES = 128
NODE_DEV = 512
LANES = 128
SIDE = 4
STRIDE = (32, 8, 2)
GAIN = 8.0

f32 = jnp.float32
bf16 = jnp.bfloat16
VMEM = pltpu.VMEM
MESH = pl.DeviceIdType.MESH


def place():
    me = lax.axis_index("dev")
    return me, lax.rem(me, 2), tuple(lax.rem(me // s, SIDE) for s in STRIDE)


def peer_of(me, spot, axis, step):
    return me + (lax.rem(spot[axis] + step, SIDE) - spot[axis]) * STRIDE[axis]


def greet(me, core, spot):
    barrier = pltpu.get_barrier_semaphore()
    for axis in range(3):
        for step in (1, 2, 3):
            peer = peer_of(me, spot, axis, step)
            pl.semaphore_signal(barrier, inc=1, device_id=(peer,), device_id_type=MESH)
    pl.semaphore_signal(barrier, inc=1, device_id=(me + 1 - 2 * core,), device_id_type=MESH)
    return barrier


def send(src, dst, send_sem, recv_sem, device):
    copy = pltpu.make_async_remote_copy(
        src_ref=src,
        dst_ref=dst,
        send_sem=send_sem,
        recv_sem=recv_sem,
        device_id=(device,),
        device_id_type=MESH,
    )
    copy.start()
    return copy


def nothing():
    pass


def gather_stages(out, place_now, sems, beside):
    me, core, spot = place_now
    send_sem, recv_sem, core_send, core_recv = sems
    for stage in range(3):
        copies = []
        for g in range(3):
            axis = (g + stage) % 3
            done = [(g + t) % 3 for t in range(stage)]
            where = tuple(slice(None) if a in done else spot[a] for a in range(3)) + (core, g)
            for step in (1, 2, 3):
                part = out.at[where]
                copies.append(
                    send(
                        part,
                        part,
                        send_sem.at[stage, g, step - 1],
                        recv_sem.at[stage, g, 3 - step],
                        peer_of(me, spot, axis, step),
                    )
                )
        beside[stage]()
        for copy in copies:
            copy.wait()
    part = out.at[:, :, :, core]
    send(part, part, core_send, core_recv, me + 1 - 2 * core).wait()


def sum_stages(terms, place_now, buffers, sems):
    me, core, spot = place_now
    core_in, s1, r2, s2, r3, s3, r4 = buffers
    send_sem, recv_sem, core_send, core_recv = sems
    part = terms.at[:, :, :, 1 - core]
    send(part, core_in, core_send, core_recv, me + 1 - 2 * core).wait()
    for a in range(SIDE):
        for g in range(3):
            s1[g, a] = terms[a, :, :, core, g] + core_in[a, :, :, g]
    sums, landed = (s1, s2, s3), (r2, r3, r4)
    totals = []
    for stage in range(3):
        src, dst = sums[stage], landed[stage]
        ahead = []
        for g in range(3):
            gone = [(g + t) % 3 for t in range(stage)]
            ahead.append([a for a in range(3) if a not in gone].index((g + stage) % 3))
        copies = []
        for g in range(3):
            axis = (g + stage) % 3
            for step in (1, 2, 3):
                to = lax.rem(spot[axis] + step, SIDE)
                copies.append(
                    send(
                        src.at[(g,) + (slice(None),) * ahead[g] + (to,)],
                        dst.at[g, 3 - step],
                        send_sem.at[stage, g, step - 1],
                        recv_sem.at[stage, g, 3 - step],
                        peer_of(me, spot, axis, step),
                    )
                )
        for g in range(3):
            axis = (g + stage) % 3
            for k in range(3):
                copies[3 * g + k].wait_recv()
            mine = (g,) + (slice(None),) * ahead[g] + (spot[axis],)
            total = (src[mine] + dst[g, 0]) + (dst[g, 1] + dst[g, 2])
            if stage < 2:
                sums[stage + 1][g] = total
            else:
                totals.append(total)
        for copy in copies:
            copy.wait_send()
    return totals


def sum_buffers(rows):
    tail = (rows, LANES)
    return [
        VMEM((4, 4, 4, 3) + tail, f32),
        VMEM((3, 4, 4, 4) + tail, f32),
        VMEM((3, 3, 4, 4) + tail, f32),
        VMEM((3, 4, 4) + tail, f32),
        VMEM((3, 3, 4) + tail, f32),
        VMEM((3, 4) + tail, f32),
        VMEM((3, 3) + tail, f32),
    ]


def stage_sems():
    dma = pltpu.SemaphoreType.DMA
    return [dma((3, 3, 3)), dma((3, 3, 3)), dma, dma]


def halves(x):
    high = x.astype(bf16)
    return high, (x - high.astype(f32)).astype(bf16)


def times_factor(values, high, low, contract):
    top, bottom = halves(values)
    both = jnp.concatenate([top, bottom], axis=0)
    dims = (((1,), (contract,)), ((), ()))
    first = lax.dot_general(both, high[...], dims, preferred_element_type=f32)
    second = lax.dot_general(both, low[...], dims, preferred_element_type=f32)
    return (first[:8] + first[8:]) + (second[:8] + second[8:])


def apply_inverse(values, high, low):
    return times_factor(times_factor(values, high, low, 1), high, low, 0)


def at_owner(ids):
    device = lax.shift_right_logical(ids[...], 9)
    return lax.broadcasted_iota(jnp.int32, (PATCHES, PN), 0) == device


def mark_local(ids, marks):
    local = lax.bitwise_and(ids[...], NODE_DEV - 1)
    found = lax.broadcasted_iota(jnp.int32, (NODE_DEV, PN), 0) == local
    marks[...] = jnp.where(found, 1.0, 0.0).astype(bf16)


def split_factor(factor, high, low):
    def step(t, _):
        part = pl.ds(pl.multiple_of(t * LANES, LANES), LANES)
        high[part, :], low[part, :] = halves(factor[part, :])
        return 0

    lax.fori_loop(0, PN // LANES, step, 0)


def factor_scratch():
    return [
        VMEM((PN, PN), f32),
        VMEM((PN, PN), bf16),
        VMEM((PN, PN), bf16),
        VMEM((NODE_DEV, PN), bf16),
        pltpu.SemaphoreType.DMA,
    ]


def patch_kernel(coords, disp, ids, factor_hbm, fluid_x, fluid_f, blend, names, *rest):
    table, fields, targets, nodes, factor, high, low, marks, factor_sem = rest[:9]
    node_sems, table_sems = rest[9:13], rest[13:17]
    me, core, spot = place()
    load = pltpu.make_async_copy(factor_hbm, factor, factor_sem)
    load.start()
    barrier = greet(me, core, spot)
    for g in range(3):
        for r in range(4):
            lanes = pl.ds(r * LANES, LANES)
            nodes[spot[0], spot[1], spot[2], core, g, pl.ds(r, 1), :] = coords[pl.ds(g, 1), lanes]
            nodes[spot[0], spot[1], spot[2], core, g, pl.ds(4 + r, 1), :] = disp[pl.ds(g, 1), lanes]
    mark_local(ids, marks)
    pl.semaphore_wait(barrier, 10)

    def fill_fields():
        x, f, b = fluid_x[...], fluid_f[...], blend[...]
        square = GAIN * jnp.sum(x * x, axis=0, keepdims=True)
        share = b / jnp.sum(b, axis=0, keepdims=True)
        for c in range(3):
            fields[c] = x[c : c + 1]
            fields[3 + c] = f[c : c + 1]
        fields[6] = square
        for s in range(SLOTS):
            fields[7 + s] = share[s : s + 1]
            targets[s] = names[pl.ds(s, 1), :]

    def ready_factor():
        load.wait()
        split_factor(factor, high, low)

    gather_stages(nodes, (me, core, spot), node_sems, (fill_fields, ready_factor, nothing))

    rows = nodes.reshape(PATCHES * 24, LANES)

    def pick(h):
        pieces = []
        for g in range(3):
            first = 8 * g + 4 * h
            row = [rows[pl.ds(first + r, PATCHES, stride=24), :] for r in range(4)]
            pieces.append(jnp.concatenate(row, axis=1))
        top, bottom = halves(jnp.concatenate(pieces, axis=0))
        found = jnp.dot(top, marks[...], preferred_element_type=f32)
        found = found + jnp.dot(bottom, marks[...], preferred_element_type=f32)
        where = at_owner(ids)
        out = []
        for g in range(3):
            mine = jnp.where(where, found[g * PATCHES : (g + 1) * PATCHES], 0.0)
            out.append(jnp.sum(mine, axis=0, keepdims=True))
        return out

    moved = jnp.concatenate(pick(1) + [jnp.zeros((5, PN), f32)], axis=0)
    coeffs = apply_inverse(moved, high, low)
    centres = pick(0)
    for g in range(3):
        scaled = centres[g] * (-2.0 * GAIN)
        for s in range(8):
            lanes = slice(s * LANES, (s + 1) * LANES)
            table[spot[0], spot[1], spot[2], core, g, pl.ds(s, 1), :] = scaled[:, lanes]
            table[spot[0], spot[1], spot[2], core, g, pl.ds(8 + s, 1), :] = coeffs[g : g + 1, lanes]
    gather_stages(table, (me, core, spot), table_sems, (nothing,) * 3)


def patch_tables(node_coords, node_disp, node_list, factor, coords, loads, blend, names):
    points = coords.shape[1]
    vmem = pl.BlockSpec(memory_space=VMEM)
    return pl.pallas_call(
        patch_kernel,
        out_shape=(
            jax.ShapeDtypeStruct((4, 4, 4, 2, 3, 16, LANES), f32),
            jax.ShapeDtypeStruct((FIELDS, 1, points), f32),
            jax.ShapeDtypeStruct((SLOTS, 1, points), jnp.int32),
        ),
        in_specs=[vmem] * 3 + [pl.BlockSpec(memory_space=pl.ANY)] + [vmem] * 4,
        out_specs=[vmem] * 3,
        scratch_shapes=[VMEM((4, 4, 4, 2, 3, 8, LANES), f32)]
        + factor_scratch()
        + stage_sems()
        + stage_sems(),
        compiler_params=pltpu.CompilerParams(
            collective_id=0, has_side_effects=True, vmem_limit_bytes=60 * 2**20
        ),
    )(node_coords, node_disp, node_list, factor, coords, loads, blend, names)


def load_kernel(terms, ids, factor_hbm, out, spread, factor, high, low, marks, factor_sem, *rest):
    patch_buffers, node_buffers = rest[:7], rest[7:14]
    patch_sems, node_sems = rest[14:18], rest[18:22]
    me, core, spot = place()
    load = pltpu.make_async_copy(factor_hbm, factor, factor_sem)
    load.start()
    barrier = greet(me, core, spot)
    mark_local(ids, marks)
    load.wait()
    split_factor(factor, high, low)
    pl.semaphore_wait(barrier, 10)
    summed = sum_stages(terms, (me, core, spot), patch_buffers, patch_sems)
    rows = [jnp.concatenate([part[s : s + 1] for s in range(8)], axis=1) for part in summed]
    rows = jnp.concatenate(rows + [jnp.zeros((5, PN), f32)], axis=0)
    loads = apply_inverse(rows * (1.0 / 32.0), high, low)
    where = at_owner(ids)
    parts = []
    for g in range(3):
        parts.extend(halves(jnp.where(where, loads[g : g + 1], 0.0)))
    found = lax.dot_general(
        jnp.concatenate(parts, axis=0),
        marks[...],
        (((1,), (1,)), ((), ())),
        preferred_element_type=f32,
    )
    flat = spread.reshape(PATCHES * 12, LANES)
    for g in range(3):
        base = 2 * g * PATCHES
        term = found[base : base + PATCHES] + found[base + PATCHES : base + 2 * PATCHES]
        for r in range(4):
            lanes = slice(r * LANES, (r + 1) * LANES)
            flat[pl.ds(4 * g + r, PATCHES, stride=12), :] = term[:, lanes]
    owned = sum_stages(spread, (me, core, spot), node_buffers, node_sems)
    for g in range(3):
        for r in range(4):
            out[pl.ds(g, 1), pl.ds(r * LANES, LANES)] = owned[g][r : r + 1]


def node_sums(terms, node_list, factor):
    vmem = pl.BlockSpec(memory_space=VMEM)
    return pl.pallas_call(
        load_kernel,
        out_shape=jax.ShapeDtypeStruct((3, NODE_DEV), f32),
        in_specs=[vmem] * 2 + [pl.BlockSpec(memory_space=pl.ANY)],
        out_specs=vmem,
        scratch_shapes=[VMEM((4, 4, 4, 2, 3, 4, LANES), f32)]
        + factor_scratch()
        + sum_buffers(8)
        + sum_buffers(4)
        + stage_sems()
        + stage_sems(),
        compiler_params=pltpu.CompilerParams(
            collective_id=1, has_side_effects=True, vmem_limit_bytes=60 * 2**20
        ),
    )(terms, node_list, factor)


FIELDS = 11


def fluid_kernel(*refs):
    patch, fields, table, disp, acc, work, sumacc, got = refs[:8]
    names, data = refs[8 : 8 + SLOTS], refs[8 + SLOTS :]
    copies = [pltpu.make_async_copy(patch.at[s], names[s], got.at[s]) for s in range(SLOTS)]
    copies += [pltpu.make_async_copy(fields.at[j], data[j], got.at[SLOTS + j]) for j in range(FIELDS)]
    for copy in copies:
        copy.start()
    points = disp.shape[1]
    lane = lax.broadcasted_iota(jnp.int32, (8, LANES), 1)

    def patch_step(p, _):
        y = [table[6 * p + 2 * c] for c in range(3)]
        total = (y[0] * y[0] + y[1] * y[1]) + y[2] * y[2]
        for c in range(3):
            work[p * 8 + c] = y[c]
            work[p * 8 + 4 + c] = table[6 * p + 2 * c + 1]
            sumacc[p * 8 + c] = jnp.zeros((8, LANES), f32)
        work[p * 8 + 3] = 1.0 + total * (1.0 / (4.0 * GAIN))
        return 0

    lax.fori_loop(0, PATCHES, patch_step, 0)

    for copy in copies:
        copy.wait()

    def block_step(block, _):
        start = block * LANES

        def point_step(group, held):
            first = group * 64
            ahead = lane - first
            held = list(held)
            for q in range(64):
                i = start + first + q
                x, y, z, square = data[0][0, i], data[1][0, i], data[2][0, i], data[6][0, i]
                ps = [names[s][0, i] * 8 for s in range(SLOTS)]
                term = []
                for s in range(SLOTS):
                    p = ps[s]
                    near = (work[p] * x + work[p + 1] * y) + (work[p + 2] * z + (work[p + 3] + square))
                    term.append(lax.rsqrt(near) * data[7 + s][0, i])
                old = [[sumacc[p + c] for c in range(3)] for p in ps]
                here = ahead == q
                for c in range(3):
                    dots = [work[ps[s] + 4 + c] * term[s] for s in range(SLOTS)]
                    value = (dots[0] + dots[1]) + (dots[2] + dots[3])
                    held[c] = jnp.where(here, jnp.sum(value, axis=1, keepdims=True), held[c])
                force = [data[3 + c][0, i] for c in range(3)]
                for s in range(SLOTS):
                    for c in range(3):
                        sumacc[ps[s] + c] = old[s][c] + term[s] * force[c]
            return tuple(held)

        held = lax.fori_loop(0, LANES // 64, point_step, (jnp.zeros((8, LANES), f32),) * 3)
        for c in range(3):
            total = jnp.sum(held[c], axis=0, keepdims=True)
            disp[pl.ds(c, 1), pl.ds(pl.multiple_of(start, LANES), LANES)] = total * (1.0 / 32.0)
        return 0

    lax.fori_loop(0, points // LANES, block_step, 0)

    def acc_step(p, _):
        for c in range(3):
            acc[3 * p + c] = sumacc[8 * p + c]
        return 0

    lax.fori_loop(0, PATCHES, acc_step, 0)


def fluid(patch, fields, table):
    points = fields.shape[2]
    return pl.pallas_call(
        fluid_kernel,
        out_shape=(
            jax.ShapeDtypeStruct((3, points), f32),
            jax.ShapeDtypeStruct((PATCHES * 3, 8, LANES), f32),
        ),
        in_specs=[pl.BlockSpec(memory_space=pl.ANY)] * 2 + [pl.BlockSpec(memory_space=VMEM)],
        out_specs=[pl.BlockSpec(memory_space=VMEM)] * 2,
        scratch_shapes=[
            VMEM((PATCHES * 8, 8, LANES), f32),
            VMEM((PATCHES * 8, 8, LANES), f32),
            pltpu.SemaphoreType.DMA((SLOTS + FIELDS,)),
        ]
        + [pltpu.SMEM((1, points), jnp.int32)] * SLOTS
        + [pltpu.SMEM((1, points), f32)] * FIELDS,
    )(patch, fields, table)


def local(node_coords, node_disp, node_list, factor, fluid_coords, fluid_loads, fluid_patch, blend_raw):
    table, fields, names = patch_tables(
        node_coords,
        node_disp,
        node_list,
        factor[0],
        fluid_coords,
        fluid_loads,
        blend_raw.T,
        fluid_patch.T,
    )
    fluid_disp, terms = fluid(names, fields, table.reshape(PATCHES * 6, 8, LANES))
    return fluid_disp, node_sums(terms.reshape(4, 4, 4, 2, 3, 8, LANES), node_list, factor[0])


def solution(mesh):
    placed = (
        P(None, "dev"),
        P(None, "dev"),
        P("dev", None),
        P("dev", None, None),
        P(None, "dev"),
        P(None, "dev"),
        P("dev", None),
        P("dev", None),
    )
    return jax.shard_map(
        local,
        mesh=mesh,
        in_specs=placed,
        out_specs=(P(None, "dev"), P(None, "dev")),
        check_vma=False,
    )
```

```python
import jax
import jax.numpy as jnp
from jax import lax
from jax.experimental import pallas as pl
from jax.experimental.pallas import tpu as pltpu
from jax.sharding import PartitionSpec as P

PN = 1024
SLOTS = 4
PATCHES = 128
NODE_DEV = 512
LANES = 128
SIDE = 4
STRIDE = (32, 8, 2)
GAIN = 8.0

f32 = jnp.float32
bf16 = jnp.bfloat16
VMEM = pltpu.VMEM
MESH = pl.DeviceIdType.MESH


def place():
    me = lax.axis_index("dev")
    return me, lax.rem(me, 2), tuple(lax.rem(me // s, SIDE) for s in STRIDE)


def peer_of(me, spot, axis, step):
    return me + (lax.rem(spot[axis] + step, SIDE) - spot[axis]) * STRIDE[axis]


def greet(me, core, spot):
    barrier = pltpu.get_barrier_semaphore()
    for axis in range(3):
        for step in (1, 2, 3):
            peer = peer_of(me, spot, axis, step)
            pl.semaphore_signal(barrier, inc=1, device_id=(peer,), device_id_type=MESH)
    pl.semaphore_signal(barrier, inc=1, device_id=(me + 1 - 2 * core,), device_id_type=MESH)
    return barrier


def send(src, dst, send_sem, recv_sem, device):
    copy = pltpu.make_async_remote_copy(
        src_ref=src,
        dst_ref=dst,
        send_sem=send_sem,
        recv_sem=recv_sem,
        device_id=(device,),
        device_id_type=MESH,
    )
    copy.start()
    return copy


def nothing():
    pass


def gather_stages(out, place_now, sems, beside, late=None):
    me, core, spot = place_now
    send_sem, recv_sem, core_send, core_recv = sems
    partner = me + 1 - 2 * core
    for stage in range(3):
        copies, passed = [], []

        def where(g, last):
            axis = (g + stage) % 3
            done = [(g + t) % 3 for t in range(stage)]
            spots = [slice(None) if a in done else spot[a] for a in range(3)]
            spots[axis] = last
            return tuple(spots) + (core, g)

        def start(rows, turn):
            for g in range(3):
                axis = (g + stage) % 3
                for step in (1, 2, 3):
                    part = out.at[where(g, spot[axis]) + rows]
                    copies.append(
                        send(
                            part,
                            part,
                            send_sem.at[turn, g, step - 1],
                            recv_sem.at[turn, g, 3 - step],
                            peer_of(me, spot, axis, step),
                        )
                    )

        if stage == 0 and late is not None:
            start((pl.ds(8, 8),), 0)
            late()
            start((pl.ds(0, 8),), 3)
        else:
            start((), stage)
        if stage < 2:
            beside[stage]()
            for copy in copies:
                copy.wait()
            continue
        for g in range(3):
            part = out.at[where(g, spot[(g + stage) % 3])]
            passed.append(send(part, part, core_send.at[g, 0], core_recv.at[g, 0], partner))
        beside[stage]()
        for k, step in enumerate((3, 1, 2)):
            for g in range(3):
                axis = (g + stage) % 3
                copies[3 * g + step - 1].wait_recv()
                part = out.at[where(g, lax.rem(spot[axis] + SIDE - step, SIDE))]
                passed.append(send(part, part, core_send.at[g, 1 + k], core_recv.at[g, 1 + k], partner))
        for copy in copies:
            copy.wait_send()
        for copy in passed:
            copy.wait()


def sum_stages(terms, place_now, buffers, sems):
    me, core, spot = place_now
    core_in, s1, r2, s2, r3, s3, r4 = buffers
    send_sem, recv_sem, core_send, core_recv = sems
    part = terms.at[:, :, :, 1 - core]
    send(part, core_in, core_send, core_recv, me + 1 - 2 * core).wait()
    for a in range(SIDE):
        for g in range(3):
            s1[g, a] = terms[a, :, :, core, g] + core_in[a, :, :, g]
    sums, landed = (s1, s2, s3), (r2, r3, r4)
    totals = []
    for stage in range(3):
        src, dst = sums[stage], landed[stage]
        ahead = []
        for g in range(3):
            gone = [(g + t) % 3 for t in range(stage)]
            ahead.append([a for a in range(3) if a not in gone].index((g + stage) % 3))
        copies = []
        for g in range(3):
            axis = (g + stage) % 3
            for step in (1, 2, 3):
                to = lax.rem(spot[axis] + step, SIDE)
                copies.append(
                    send(
                        src.at[(g,) + (slice(None),) * ahead[g] + (to,)],
                        dst.at[g, 3 - step],
                        send_sem.at[stage, g, step - 1],
                        recv_sem.at[stage, g, 3 - step],
                        peer_of(me, spot, axis, step),
                    )
                )
        for g in range(3):
            axis = (g + stage) % 3
            for k in range(3):
                copies[3 * g + k].wait_recv()
            mine = (g,) + (slice(None),) * ahead[g] + (spot[axis],)
            total = (src[mine] + dst[g, 0]) + (dst[g, 1] + dst[g, 2])
            if stage < 2:
                sums[stage + 1][g] = total
            else:
                totals.append(total)
        for copy in copies:
            copy.wait_send()
    return totals


def sum_buffers(rows):
    tail = (rows, LANES)
    return [
        VMEM((4, 4, 4, 3) + tail, f32),
        VMEM((3, 4, 4, 4) + tail, f32),
        VMEM((3, 3, 4, 4) + tail, f32),
        VMEM((3, 4, 4) + tail, f32),
        VMEM((3, 3, 4) + tail, f32),
        VMEM((3, 4) + tail, f32),
        VMEM((3, 3) + tail, f32),
    ]


def stage_sems(gather):
    dma = pltpu.SemaphoreType.DMA
    if gather:
        return [dma((4, 3, 3)), dma((4, 3, 3)), dma((3, 4)), dma((3, 4))]
    return [dma((3, 3, 3)), dma((3, 3, 3)), dma, dma]


def halves(x):
    high = x.astype(bf16)
    return high, (x - high.astype(f32)).astype(bf16)


def times_factor(values, high, low, contract):
    top, bottom = halves(values)
    both = jnp.concatenate([top, bottom], axis=0)
    dims = (((1,), (contract,)), ((), ()))
    first = lax.dot_general(both, high[...], dims, preferred_element_type=f32)
    second = lax.dot_general(both, low[...], dims, preferred_element_type=f32)
    return (first[:8] + first[8:]) + (second[:8] + second[8:])


def apply_inverse(values, high, low):
    return times_factor(times_factor(values, high, low, 1), high, low, 0)


def at_owner(ids):
    device = lax.shift_right_logical(ids[...], 9)
    return lax.broadcasted_iota(jnp.int32, (PATCHES, PN), 0) == device


def mark_local(ids, marks):
    local = lax.bitwise_and(ids[...], NODE_DEV - 1)
    found = lax.broadcasted_iota(jnp.int32, (NODE_DEV, PN), 0) == local
    marks[...] = jnp.where(found, 1.0, 0.0).astype(bf16)


def split_factor(factor, high, low):
    def step(t, _):
        part = pl.ds(pl.multiple_of(t * LANES, LANES), LANES)
        high[part, :], low[part, :] = halves(factor[part, :])
        return 0

    lax.fori_loop(0, PN // LANES, step, 0)


def factor_scratch():
    return [
        VMEM((PN, PN), f32),
        VMEM((PN, PN), bf16),
        VMEM((PN, PN), bf16),
        VMEM((NODE_DEV, PN), bf16),
        pltpu.SemaphoreType.DMA,
    ]


def patch_kernel(coords, disp, ids, factor_hbm, fluid_x, fluid_f, blend, names, *rest):
    table, fields, targets, nodes, factor, high, low, marks, factor_sem = rest[:9]
    node_sems, table_sems = rest[9:13], rest[13:17]
    me, core, spot = place()
    load = pltpu.make_async_copy(factor_hbm, factor, factor_sem)
    load.start()
    barrier = greet(me, core, spot)
    for g in range(3):
        for r in range(4):
            lanes = pl.ds(r * LANES, LANES)
            nodes[spot[0], spot[1], spot[2], core, g, pl.ds(r, 1), :] = coords[pl.ds(g, 1), lanes]
            nodes[spot[0], spot[1], spot[2], core, g, pl.ds(4 + r, 1), :] = disp[pl.ds(g, 1), lanes]
    mark_local(ids, marks)
    pl.semaphore_wait(barrier, 10)

    def fill_fields():
        x, f, b = fluid_x[...], fluid_f[...], blend[...]
        square = GAIN * jnp.sum(x * x, axis=0, keepdims=True)
        share = b / jnp.sum(b, axis=0, keepdims=True)
        for c in range(3):
            fields[c] = x[c : c + 1]
            fields[3 + c] = f[c : c + 1]
        fields[6] = square
        for s in range(SLOTS):
            fields[7 + s] = share[s : s + 1]
            targets[s] = names[pl.ds(s, 1), :]

    def ready_factor():
        load.wait()
        split_factor(factor, high, low)

    gather_stages(nodes, (me, core, spot), node_sems, (fill_fields, ready_factor, nothing))

    rows = nodes.reshape(PATCHES * 24, LANES)

    def pick(h):
        pieces = []
        for g in range(3):
            first = 8 * g + 4 * h
            row = [rows[pl.ds(first + r, PATCHES, stride=24), :] for r in range(4)]
            pieces.append(jnp.concatenate(row, axis=1))
        top, bottom = halves(jnp.concatenate(pieces, axis=0))
        found = jnp.dot(top, marks[...], preferred_element_type=f32)
        found = found + jnp.dot(bottom, marks[...], preferred_element_type=f32)
        where = at_owner(ids)
        out = []
        for g in range(3):
            mine = jnp.where(where, found[g * PATCHES : (g + 1) * PATCHES], 0.0)
            out.append(jnp.sum(mine, axis=0, keepdims=True))
        return out

    moved = jnp.concatenate(pick(1) + [jnp.zeros((5, PN), f32)], axis=0)
    coeffs = apply_inverse(moved, high, low)

    def fill(values, first):
        for g in range(3):
            for s in range(8):
                lanes = slice(s * LANES, (s + 1) * LANES)
                table[spot[0], spot[1], spot[2], core, g, pl.ds(first + s, 1), :] = values[g][:, lanes]

    def fill_centres():
        fill([y * (-2.0 * GAIN) for y in pick(0)], 0)

    fill([coeffs[g : g + 1] for g in range(3)], 8)
    gather_stages(table, (me, core, spot), table_sems, (nothing,) * 3, fill_centres)


def patch_tables(node_coords, node_disp, node_list, factor, coords, loads, blend, names):
    points = coords.shape[1]
    vmem = pl.BlockSpec(memory_space=VMEM)
    return pl.pallas_call(
        patch_kernel,
        out_shape=(
            jax.ShapeDtypeStruct((4, 4, 4, 2, 3, 16, LANES), f32),
            jax.ShapeDtypeStruct((FIELDS, 1, points), f32),
            jax.ShapeDtypeStruct((SLOTS, 1, points), jnp.int32),
        ),
        in_specs=[vmem] * 3 + [pl.BlockSpec(memory_space=pl.ANY)] + [vmem] * 4,
        out_specs=[vmem] * 3,
        scratch_shapes=[VMEM((4, 4, 4, 2, 3, 8, LANES), f32)]
        + factor_scratch()
        + stage_sems(True)
        + stage_sems(True),
        compiler_params=pltpu.CompilerParams(
            collective_id=0, has_side_effects=True, vmem_limit_bytes=60 * 2**20
        ),
    )(node_coords, node_disp, node_list, factor, coords, loads, blend, names)


def load_kernel(terms_hbm, ids, factor_hbm, out, spread, factor, high, low, marks, factor_sem, terms, terms_sem, *rest):
    patch_buffers, node_buffers = rest[:7], rest[7:14]
    patch_sems, node_sems = rest[14:18], rest[18:22]
    me, core, spot = place()
    load = pltpu.make_async_copy(factor_hbm, factor, factor_sem)
    fill = pltpu.make_async_copy(terms_hbm, terms, terms_sem)
    fill.start()
    load.start()
    barrier = greet(me, core, spot)
    mark_local(ids, marks)
    load.wait()
    split_factor(factor, high, low)
    fill.wait()
    pl.semaphore_wait(barrier, 10)
    summed = sum_stages(terms, (me, core, spot), patch_buffers, patch_sems)
    rows = [jnp.concatenate([part[s : s + 1] for s in range(8)], axis=1) for part in summed]
    rows = jnp.concatenate(rows + [jnp.zeros((5, PN), f32)], axis=0)
    loads = apply_inverse(rows * (1.0 / 32.0), high, low)
    where = at_owner(ids)
    parts = []
    for g in range(3):
        parts.extend(halves(jnp.where(where, loads[g : g + 1], 0.0)))
    found = lax.dot_general(
        jnp.concatenate(parts, axis=0),
        marks[...],
        (((1,), (1,)), ((), ())),
        preferred_element_type=f32,
    )
    flat = spread.reshape(PATCHES * 12, LANES)
    for g in range(3):
        base = 2 * g * PATCHES
        term = found[base : base + PATCHES] + found[base + PATCHES : base + 2 * PATCHES]
        for r in range(4):
            lanes = slice(r * LANES, (r + 1) * LANES)
            flat[pl.ds(4 * g + r, PATCHES, stride=12), :] = term[:, lanes]
    owned = sum_stages(spread, (me, core, spot), node_buffers, node_sems)
    for g in range(3):
        for r in range(4):
            out[pl.ds(g, 1), pl.ds(r * LANES, LANES)] = owned[g][r : r + 1]


def node_sums(terms, node_list, factor):
    vmem = pl.BlockSpec(memory_space=VMEM)
    hbm = pl.BlockSpec(memory_space=pl.ANY)
    return pl.pallas_call(
        load_kernel,
        out_shape=jax.ShapeDtypeStruct((3, NODE_DEV), f32),
        in_specs=[hbm, vmem, hbm],
        out_specs=vmem,
        scratch_shapes=[VMEM((4, 4, 4, 2, 3, 4, LANES), f32)]
        + factor_scratch()
        + [VMEM((4, 4, 4, 2, 3, 8, LANES), f32), pltpu.SemaphoreType.DMA]
        + sum_buffers(8)
        + sum_buffers(4)
        + stage_sems(False)
        + stage_sems(False),
        compiler_params=pltpu.CompilerParams(
            collective_id=1, has_side_effects=True, vmem_limit_bytes=60 * 2**20
        ),
    )(terms, node_list, factor)


FIELDS = 11


def fluid_kernel(*refs):
    patch, fields, table_hbm, disp, acc, work, table, table_sem, got = refs[:9]
    names, data = refs[9 : 9 + SLOTS], refs[9 + SLOTS :]
    fill = pltpu.make_async_copy(table_hbm, table, table_sem)
    fill.start()
    copies = [pltpu.make_async_copy(patch.at[s], names[s], got.at[s]) for s in range(SLOTS)]
    copies += [pltpu.make_async_copy(fields.at[j], data[j], got.at[SLOTS + j]) for j in range(FIELDS)]
    for copy in copies:
        copy.start()
    points = disp.shape[1]
    lane = lax.broadcasted_iota(jnp.int32, (8, LANES), 1)

    def patch_step(p, _):
        y = [table[6 * p + 2 * c] for c in range(3)]
        total = (y[0] * y[0] + y[1] * y[1]) + y[2] * y[2]
        for c in range(3):
            work[p * 8 + c] = y[c]
            work[p * 8 + 4 + c] = table[6 * p + 2 * c + 1]
            acc[p * 3 + c] = jnp.zeros((8, LANES), f32)
        work[p * 8 + 3] = 1.0 + total * (1.0 / (4.0 * GAIN))
        return 0

    fill.wait()
    lax.fori_loop(0, PATCHES, patch_step, 0)

    for copy in copies:
        copy.wait()

    def block_step(block, _):
        start = block * LANES

        def point_step(group, held):
            first = group * 64
            ahead = lane - first
            held = list(held)
            for q in range(64):
                i = start + first + q
                x, y, z, square = data[0][0, i], data[1][0, i], data[2][0, i], data[6][0, i]
                ps = [names[s][0, i] for s in range(SLOTS)]
                term = []
                for s in range(SLOTS):
                    p = ps[s] * 8
                    near = (work[p] * x + work[p + 1] * y) + (work[p + 2] * z + (work[p + 3] + square))
                    term.append(lax.rsqrt(near) * data[7 + s][0, i])
                old = [[acc[p * 3 + c] for c in range(3)] for p in ps]
                here = ahead == q
                for c in range(3):
                    dots = [work[ps[s] * 8 + 4 + c] * term[s] for s in range(SLOTS)]
                    value = (dots[0] + dots[1]) + (dots[2] + dots[3])
                    held[c] = jnp.where(here, jnp.sum(value, axis=1, keepdims=True), held[c])
                force = [data[3 + c][0, i] for c in range(3)]
                for s in range(SLOTS):
                    for c in range(3):
                        acc[ps[s] * 3 + c] = old[s][c] + term[s] * force[c]
            return tuple(held)

        held = lax.fori_loop(0, LANES // 64, point_step, (jnp.zeros((8, LANES), f32),) * 3)
        for c in range(3):
            total = jnp.sum(held[c], axis=0, keepdims=True)
            disp[pl.ds(c, 1), pl.ds(pl.multiple_of(start, LANES), LANES)] = total * (1.0 / 32.0)
        return 0

    lax.fori_loop(0, points // LANES, block_step, 0)


def fluid(patch, fields, table):
    points = fields.shape[2]
    return pl.pallas_call(
        fluid_kernel,
        out_shape=(
            jax.ShapeDtypeStruct((3, points), f32),
            jax.ShapeDtypeStruct((PATCHES * 3, 8, LANES), f32),
        ),
        in_specs=[pl.BlockSpec(memory_space=pl.ANY)] * 3,
        out_specs=[pl.BlockSpec(memory_space=VMEM)] * 2,
        scratch_shapes=[
            VMEM((PATCHES * 8, 8, LANES), f32),
            VMEM((PATCHES * 6, 8, LANES), f32),
            pltpu.SemaphoreType.DMA,
            pltpu.SemaphoreType.DMA((SLOTS + FIELDS,)),
        ]
        + [pltpu.SMEM((1, points), jnp.int32)] * SLOTS
        + [pltpu.SMEM((1, points), f32)] * FIELDS,
    )(patch, fields, table)


def local(node_coords, node_disp, node_list, factor, fluid_coords, fluid_loads, fluid_patch, blend_raw):
    table, fields, names = patch_tables(
        node_coords,
        node_disp,
        node_list,
        factor[0],
        fluid_coords,
        fluid_loads,
        blend_raw.T,
        fluid_patch.T,
    )
    fluid_disp, terms = fluid(names, fields, table.reshape(PATCHES * 6, 8, LANES))
    return fluid_disp, node_sums(terms.reshape(4, 4, 4, 2, 3, 8, LANES), node_list, factor[0])


def solution(mesh):
    placed = (
        P(None, "dev"),
        P(None, "dev"),
        P("dev", None),
        P("dev", None, None),
        P(None, "dev"),
        P(None, "dev"),
        P("dev", None),
        P("dev", None),
    )
    return jax.shard_map(
        local,
        mesh=mesh,
        in_specs=placed,
        out_specs=(P(None, "dev"), P(None, "dev")),
        check_vma=False,
    )
```

```python
import jax
import jax.numpy as jnp
from jax import lax
from jax.experimental import pallas as pl
from jax.experimental.pallas import tpu as pltpu
from jax.sharding import PartitionSpec as P

PN = 1024
SLOTS = 4
PATCHES = 128
NODE_DEV = 512
LANES = 128
SIDE = 4
STRIDE = (32, 8, 2)
GAIN = 8.0

f32 = jnp.float32
bf16 = jnp.bfloat16
VMEM = pltpu.VMEM
MESH = pl.DeviceIdType.MESH


def place():
    me = lax.axis_index("dev")
    return me, lax.rem(me, 2), tuple(lax.rem(me // s, SIDE) for s in STRIDE)


def peer_of(me, spot, axis, step):
    return me + (lax.rem(spot[axis] + step, SIDE) - spot[axis]) * STRIDE[axis]


def plane_peers(me, spot, axes):
    steps = [(a, b) for a in range(SIDE) for b in range(SIDE) if a or b]
    steps.sort(key=lambda ab: min(ab[0], SIDE - ab[0]) + min(ab[1], SIDE - ab[1]))
    out = []
    for a, b in steps:
        device = peer_of(peer_of(me, spot, axes[0], a), spot, axes[1], b)
        out.append((device, (a, b), ((SIDE - a) % SIDE) * SIDE + (SIDE - b) % SIDE))
    return out


LINES = 3 * 3 + 1
PLANES = 3 * 3 + 3 * 9 + 1


def greet(me, core, spot, planes):
    barrier = pltpu.get_barrier_semaphore()
    peers = [me + 1 - 2 * core]
    for g in range(3):
        near = plane_peers(me, spot, (g, (g + 1) % 3))
        peers += [d for d, (a, b), _ in near if a and (planes or not b)]
    for peer in peers:
        pl.semaphore_signal(barrier, inc=1, device_id=(peer,), device_id_type=MESH)
    return barrier


def send(src, dst, send_sem, recv_sem, device):
    copy = pltpu.make_async_remote_copy(
        src_ref=src,
        dst_ref=dst,
        send_sem=send_sem,
        recv_sem=recv_sem,
        device_id=(device,),
        device_id_type=MESH,
    )
    copy.start()
    return copy


def nothing():
    pass


def gather_stages(out, place_now, sems, beside, late=None):
    me, core, spot = place_now
    send_sem, recv_sem, core_send, core_recv = sems
    partner = me + 1 - 2 * core
    for stage in range(3):
        copies, passed = [], []

        def where(g, last):
            axis = (g + stage) % 3
            done = [(g + t) % 3 for t in range(stage)]
            spots = [slice(None) if a in done else spot[a] for a in range(3)]
            spots[axis] = last
            return tuple(spots) + (core, g)

        def start(rows, turn):
            for g in range(3):
                axis = (g + stage) % 3
                for step in (1, 2, 3):
                    part = out.at[where(g, spot[axis]) + rows]
                    copies.append(
                        send(
                            part,
                            part,
                            send_sem.at[turn, g, step - 1],
                            recv_sem.at[turn, g, 3 - step],
                            peer_of(me, spot, axis, step),
                        )
                    )

        if stage == 0 and late is not None:
            start((pl.ds(8, 8),), 0)
            late()
            start((pl.ds(0, 8),), 3)
        else:
            start((), stage)
        if stage < 2:
            beside[stage]()
            for copy in copies:
                copy.wait()
            continue
        for g in range(3):
            part = out.at[where(g, spot[(g + stage) % 3])]
            passed.append(send(part, part, core_send.at[g, 0], core_recv.at[g, 0], partner))
        beside[stage]()
        for k, step in enumerate((3, 1, 2)):
            for g in range(3):
                axis = (g + stage) % 3
                copies[3 * g + step - 1].wait_recv()
                part = out.at[where(g, lax.rem(spot[axis] + SIDE - step, SIDE))]
                passed.append(send(part, part, core_send.at[g, 1 + k], core_recv.at[g, 1 + k], partner))
        for copy in copies:
            copy.wait_send()
        for copy in passed:
            copy.wait()


def sum_stages(terms, place_now, buffers, sems):
    me, core, spot = place_now
    core_in, s1, r2, s2, r3 = buffers
    plane_send, plane_recv, line_send, line_recv, core_send, core_recv = sems
    part = terms.at[:, :, :, 1 - core]
    send(part, core_in, core_send, core_recv, me + 1 - 2 * core).wait()
    for a in range(SIDE):
        for g in range(3):
            s1[g, a] = terms[a, :, :, core, g] + core_in[a, :, :, g]
    copies = []
    for g in range(3):
        for step in (1, 2, 3):
            to = lax.rem(spot[g] + step, SIDE)
            copies.append(
                send(
                    s1.at[(g,) + (slice(None),) * g + (to,)],
                    r2.at[g, 3 - step],
                    line_send.at[g, step - 1],
                    line_recv.at[g, 3 - step],
                    peer_of(me, spot, g, step),
                )
            )
    for g in range(3):
        for k in range(3):
            copies[3 * g + k].wait_recv()
        mine = (g,) + (slice(None),) * g + (spot[g],)
        s2[g] = (s1[mine] + r2[g, 0]) + (r2[g, 1] + r2[g, 2])
    left = [[a for a in range(3) if a != g] for g in range(3)]
    around = [plane_peers(me, spot, left[g]) for g in range(3)]
    spread = [[], [], []]
    for k in range(15):
        for g in range(3):
            device, (a, b), there = around[g][k]
            to = (lax.rem(spot[left[g][0]] + a, SIDE), lax.rem(spot[left[g][1]] + b, SIDE))
            spread[g].append(
                send(
                    s2.at[(g,) + to],
                    r3.at[g, there],
                    plane_send.at[g, SIDE * a + b],
                    plane_recv.at[g, there],
                    device,
                )
            )
    totals = []
    for g in range(3):
        for copy in spread[g]:
            copy.wait_recv()
        terms_now = [s2[g, spot[left[g][0]], spot[left[g][1]]]] + [r3[g, k] for k in range(1, 16)]
        while len(terms_now) > 1:
            terms_now = [x + y for x, y in zip(terms_now[::2], terms_now[1::2])]
        totals.append(terms_now[0])
    for copy in copies + spread[0] + spread[1] + spread[2]:
        copy.wait_send()
    return totals


def sum_buffers(rows):
    tail = (rows, LANES)
    return [
        VMEM((4, 4, 4, 3) + tail, f32),
        VMEM((3, 4, 4, 4) + tail, f32),
        VMEM((3, 3, 4, 4) + tail, f32),
        VMEM((3, 4, 4) + tail, f32),
        VMEM((3, 16) + tail, f32),
    ]


def stage_sems(gather):
    dma = pltpu.SemaphoreType.DMA
    if gather:
        return [dma((4, 3, 3)), dma((4, 3, 3)), dma((3, 4)), dma((3, 4))]
    return [dma((3, 16)), dma((3, 16)), dma((3, 3)), dma((3, 3)), dma, dma]


def halves(x):
    high = x.astype(bf16)
    return high, (x - high.astype(f32)).astype(bf16)


def times_factor(values, high, low, contract):
    top, bottom = halves(values)
    both = jnp.concatenate([top, bottom], axis=0)
    dims = (((1,), (contract,)), ((), ()))
    first = lax.dot_general(both, high[...], dims, preferred_element_type=f32)
    second = lax.dot_general(both, low[...], dims, preferred_element_type=f32)
    return (first[:8] + first[8:]) + (second[:8] + second[8:])


def apply_inverse(values, high, low):
    return times_factor(times_factor(values, high, low, 1), high, low, 0)


def at_owner(ids):
    device = lax.shift_right_logical(ids[...], 9)
    return lax.broadcasted_iota(jnp.int32, (PATCHES, PN), 0) == device


def mark_local(ids, marks):
    local = lax.bitwise_and(ids[...], NODE_DEV - 1)
    found = lax.broadcasted_iota(jnp.int32, (NODE_DEV, PN), 0) == local
    marks[...] = jnp.where(found, 1.0, 0.0).astype(bf16)


def split_factor(factor, high, low):
    def step(t, _):
        part = pl.ds(pl.multiple_of(t * LANES, LANES), LANES)
        high[part, :], low[part, :] = halves(factor[part, :])
        return 0

    lax.fori_loop(0, PN // LANES, step, 0)


def factor_scratch():
    return [
        VMEM((PN, PN), f32),
        VMEM((PN, PN), bf16),
        VMEM((PN, PN), bf16),
        VMEM((NODE_DEV, PN), bf16),
        pltpu.SemaphoreType.DMA,
    ]


def patch_kernel(coords, disp, ids, factor_hbm, fluid_x, fluid_f, blend, names, *rest):
    table, fields, targets, nodes, factor, high, low, marks, factor_sem = rest[:9]
    node_sems, table_sems = rest[9:13], rest[13:17]
    me, core, spot = place()
    load = pltpu.make_async_copy(factor_hbm, factor, factor_sem)
    load.start()
    barrier = greet(me, core, spot, False)
    for g in range(3):
        for r in range(4):
            lanes = pl.ds(r * LANES, LANES)
            nodes[spot[0], spot[1], spot[2], core, g, pl.ds(r, 1), :] = coords[pl.ds(g, 1), lanes]
            nodes[spot[0], spot[1], spot[2], core, g, pl.ds(4 + r, 1), :] = disp[pl.ds(g, 1), lanes]
    mark_local(ids, marks)
    pl.semaphore_wait(barrier, LINES)

    def fill_fields():
        x, f, b = fluid_x[...], fluid_f[...], blend[...]
        square = GAIN * jnp.sum(x * x, axis=0, keepdims=True)
        share = b / jnp.sum(b, axis=0, keepdims=True)
        for c in range(3):
            fields[c] = x[c : c + 1]
            fields[3 + c] = f[c : c + 1]
        fields[6] = square
        for s in range(SLOTS):
            fields[7 + s] = share[s : s + 1]
            targets[s] = names[pl.ds(s, 1), :]

    def ready_factor():
        load.wait()
        split_factor(factor, high, low)

    gather_stages(nodes, (me, core, spot), node_sems, (fill_fields, ready_factor, nothing))

    rows = nodes.reshape(PATCHES * 24, LANES)

    def pick(h):
        pieces = []
        for g in range(3):
            first = 8 * g + 4 * h
            row = [rows[pl.ds(first + r, PATCHES, stride=24), :] for r in range(4)]
            pieces.append(jnp.concatenate(row, axis=1))
        top, bottom = halves(jnp.concatenate(pieces, axis=0))
        found = jnp.dot(top, marks[...], preferred_element_type=f32)
        found = found + jnp.dot(bottom, marks[...], preferred_element_type=f32)
        where = at_owner(ids)
        out = []
        for g in range(3):
            mine = jnp.where(where, found[g * PATCHES : (g + 1) * PATCHES], 0.0)
            out.append(jnp.sum(mine, axis=0, keepdims=True))
        return out

    moved = jnp.concatenate(pick(1) + [jnp.zeros((5, PN), f32)], axis=0)
    coeffs = apply_inverse(moved, high, low)

    def fill(values, first):
        for g in range(3):
            for s in range(8):
                lanes = slice(s * LANES, (s + 1) * LANES)
                table[spot[0], spot[1], spot[2], core, g, pl.ds(first + s, 1), :] = values[g][:, lanes]

    def fill_centres():
        fill([y * (-2.0 * GAIN) for y in pick(0)], 0)

    fill([coeffs[g : g + 1] for g in range(3)], 8)
    gather_stages(table, (me, core, spot), table_sems, (nothing,) * 3, fill_centres)


def patch_tables(node_coords, node_disp, node_list, factor, coords, loads, blend, names):
    points = coords.shape[1]
    vmem = pl.BlockSpec(memory_space=VMEM)
    return pl.pallas_call(
        patch_kernel,
        out_shape=(
            jax.ShapeDtypeStruct((4, 4, 4, 2, 3, 16, LANES), f32),
            jax.ShapeDtypeStruct((FIELDS, 1, points), f32),
            jax.ShapeDtypeStruct((SLOTS, 1, points), jnp.int32),
        ),
        in_specs=[vmem] * 3 + [pl.BlockSpec(memory_space=pl.ANY)] + [vmem] * 4,
        out_specs=[vmem] * 3,
        scratch_shapes=[VMEM((4, 4, 4, 2, 3, 8, LANES), f32)]
        + factor_scratch()
        + stage_sems(True)
        + stage_sems(True),
        compiler_params=pltpu.CompilerParams(
            collective_id=0, has_side_effects=True, vmem_limit_bytes=60 * 2**20
        ),
    )(node_coords, node_disp, node_list, factor, coords, loads, blend, names)


def load_kernel(terms_hbm, ids, factor_hbm, out, spread, factor, high, low, marks, factor_sem, terms, terms_sem, *rest):
    patch_buffers, node_buffers = rest[:5], rest[5:10]
    patch_sems, node_sems = rest[10:16], rest[16:22]
    me, core, spot = place()
    load = pltpu.make_async_copy(factor_hbm, factor, factor_sem)
    fill = pltpu.make_async_copy(terms_hbm, terms, terms_sem)
    fill.start()
    load.start()
    barrier = greet(me, core, spot, True)
    mark_local(ids, marks)
    load.wait()
    split_factor(factor, high, low)
    fill.wait()
    pl.semaphore_wait(barrier, PLANES)
    summed = sum_stages(terms, (me, core, spot), patch_buffers, patch_sems)
    rows = [jnp.concatenate([part[s : s + 1] for s in range(8)], axis=1) for part in summed]
    rows = jnp.concatenate(rows + [jnp.zeros((5, PN), f32)], axis=0)
    loads = apply_inverse(rows * (1.0 / 32.0), high, low)
    where = at_owner(ids)
    parts = []
    for g in range(3):
        parts.extend(halves(jnp.where(where, loads[g : g + 1], 0.0)))
    found = lax.dot_general(
        jnp.concatenate(parts, axis=0),
        marks[...],
        (((1,), (1,)), ((), ())),
        preferred_element_type=f32,
    )
    flat = spread.reshape(PATCHES * 12, LANES)
    for g in range(3):
        base = 2 * g * PATCHES
        term = found[base : base + PATCHES] + found[base + PATCHES : base + 2 * PATCHES]
        for r in range(4):
            lanes = slice(r * LANES, (r + 1) * LANES)
            flat[pl.ds(4 * g + r, PATCHES, stride=12), :] = term[:, lanes]
    owned = sum_stages(spread, (me, core, spot), node_buffers, node_sems)
    for g in range(3):
        for r in range(4):
            out[pl.ds(g, 1), pl.ds(r * LANES, LANES)] = owned[g][r : r + 1]


def node_sums(terms, node_list, factor):
    vmem = pl.BlockSpec(memory_space=VMEM)
    hbm = pl.BlockSpec(memory_space=pl.ANY)
    return pl.pallas_call(
        load_kernel,
        out_shape=jax.ShapeDtypeStruct((3, NODE_DEV), f32),
        in_specs=[hbm, vmem, hbm],
        out_specs=vmem,
        scratch_shapes=[VMEM((4, 4, 4, 2, 3, 4, LANES), f32)]
        + factor_scratch()
        + [VMEM((4, 4, 4, 2, 3, 8, LANES), f32), pltpu.SemaphoreType.DMA]
        + sum_buffers(8)
        + sum_buffers(4)
        + stage_sems(False)
        + stage_sems(False),
        compiler_params=pltpu.CompilerParams(
            collective_id=1, has_side_effects=True, vmem_limit_bytes=60 * 2**20
        ),
    )(terms, node_list, factor)


FIELDS = 11
EARLY = 4


def fluid_kernel(*refs):
    patch, fields, table_hbm, disp, acc, work, table, table_sem, got = refs[:9]
    names, data = refs[9 : 9 + SLOTS], refs[9 + SLOTS :]
    fill = pltpu.make_async_copy(table_hbm, table, table_sem)
    fill.start()
    points = disp.shape[1]
    rows = [(patch.at[s], names[s]) for s in range(SLOTS)]
    rows += [(fields.at[j], data[j]) for j in range(FIELDS)]

    def scalars(k):
        first = EARLY * LANES
        where = (slice(None), pl.ds(first, points - first) if k else pl.ds(0, first))
        return [
            pltpu.make_async_copy(src.at[where], dst.at[where], got.at[k, j])
            for j, (src, dst) in enumerate(rows)
        ]

    for k in range(2):
        for copy in scalars(k):
            copy.start()
    lane = lax.broadcasted_iota(jnp.int32, (8, LANES), 1)

    def patch_step(p, _):
        y = [table[6 * p + 2 * c] for c in range(3)]
        total = (y[0] * y[0] + y[1] * y[1]) + y[2] * y[2]
        for c in range(3):
            work[p * 8 + c] = y[c]
            work[p * 8 + 4 + c] = table[6 * p + 2 * c + 1]
            acc[p * 3 + c] = jnp.zeros((8, LANES), f32)
        work[p * 8 + 3] = 1.0 + total * (1.0 / (4.0 * GAIN))
        return 0

    fill.wait()
    lax.fori_loop(0, PATCHES, patch_step, 0)

    for copy in scalars(0):
        copy.wait()

    def block_step(block, _):
        start = block * LANES

        @pl.when(block == EARLY)
        def _():
            for copy in scalars(1):
                copy.wait()

        def point_step(group, held):
            first = group * 128
            ahead = lane - first
            held = list(held)
            for q in range(128):
                i = start + first + q
                x, y, z, square = data[0][0, i], data[1][0, i], data[2][0, i], data[6][0, i]
                ps = [names[s][0, i] for s in range(SLOTS)]
                term = []
                for s in range(SLOTS):
                    p = ps[s] * 8
                    near = (work[p] * x + work[p + 1] * y) + (work[p + 2] * z + (work[p + 3] + square))
                    term.append(lax.rsqrt(near) * data[7 + s][0, i])
                old = [[acc[p * 3 + c] for c in range(3)] for p in ps]
                here = ahead == q
                for c in range(3):
                    dots = [work[ps[s] * 8 + 4 + c] * term[s] for s in range(SLOTS)]
                    value = (dots[0] + dots[1]) + (dots[2] + dots[3])
                    held[c] = jnp.where(here, jnp.sum(value, axis=1, keepdims=True), held[c])
                force = [data[3 + c][0, i] for c in range(3)]
                for s in range(SLOTS):
                    for c in range(3):
                        acc[ps[s] * 3 + c] = old[s][c] + term[s] * force[c]
            return tuple(held)

        held = lax.fori_loop(0, LANES // 128, point_step, (jnp.zeros((8, LANES), f32),) * 3)
        for c in range(3):
            total = jnp.sum(held[c], axis=0, keepdims=True)
            disp[pl.ds(c, 1), pl.ds(pl.multiple_of(start, LANES), LANES)] = total * (1.0 / 32.0)
        return 0

    lax.fori_loop(0, points // LANES, block_step, 0)


def fluid(patch, fields, table):
    points = fields.shape[2]
    return pl.pallas_call(
        fluid_kernel,
        out_shape=(
            jax.ShapeDtypeStruct((3, points), f32),
            jax.ShapeDtypeStruct((PATCHES * 3, 8, LANES), f32),
        ),
        in_specs=[pl.BlockSpec(memory_space=pl.ANY)] * 3,
        out_specs=[pl.BlockSpec(memory_space=VMEM)] * 2,
        scratch_shapes=[
            VMEM((PATCHES * 8, 8, LANES), f32),
            VMEM((PATCHES * 6, 8, LANES), f32),
            pltpu.SemaphoreType.DMA,
            pltpu.SemaphoreType.DMA((2, SLOTS + FIELDS)),
        ]
        + [pltpu.SMEM((1, points), jnp.int32)] * SLOTS
        + [pltpu.SMEM((1, points), f32)] * FIELDS,
    )(patch, fields, table)


def local(node_coords, node_disp, node_list, factor, fluid_coords, fluid_loads, fluid_patch, blend_raw):
    table, fields, names = patch_tables(
        node_coords,
        node_disp,
        node_list,
        factor[0],
        fluid_coords,
        fluid_loads,
        blend_raw.T,
        fluid_patch.T,
    )
    fluid_disp, terms = fluid(names, fields, table.reshape(PATCHES * 6, 8, LANES))
    return fluid_disp, node_sums(terms.reshape(4, 4, 4, 2, 3, 8, LANES), node_list, factor[0])


def solution(mesh):
    placed = (
        P(None, "dev"),
        P(None, "dev"),
        P("dev", None),
        P("dev", None, None),
        P(None, "dev"),
        P(None, "dev"),
        P("dev", None),
        P("dev", None),
    )
    return jax.shard_map(
        local,
        mesh=mesh,
        in_specs=placed,
        out_specs=(P(None, "dev"), P(None, "dev")),
        check_vma=False,
    )
```

```python
import jax
import jax.numpy as jnp
from jax import lax
from jax.experimental import pallas as pl
from jax.experimental.pallas import tpu as pltpu
from jax.sharding import PartitionSpec as P

PN = 1024
SLOTS = 4
PATCHES = 128
NODE_DEV = 512
LANES = 128
SIDE = 4
STRIDE = (32, 8, 2)
GAIN = 8.0

f32 = jnp.float32
bf16 = jnp.bfloat16
VMEM = pltpu.VMEM
MESH = pl.DeviceIdType.MESH


def place():
    me = lax.axis_index("dev")
    return me, lax.rem(me, 2), tuple(lax.rem(me // s, SIDE) for s in STRIDE)


def peer_of(me, spot, axis, step):
    return me + (lax.rem(spot[axis] + step, SIDE) - spot[axis]) * STRIDE[axis]


def plane_peers(me, spot, axes):
    steps = [(a, b) for a in range(SIDE) for b in range(SIDE) if a or b]
    steps.sort(key=lambda ab: min(ab[0], SIDE - ab[0]) + min(ab[1], SIDE - ab[1]))
    out = []
    for a, b in steps:
        device = peer_of(peer_of(me, spot, axes[0], a), spot, axes[1], b)
        out.append((device, (a, b), ((SIDE - a) % SIDE) * SIDE + (SIDE - b) % SIDE))
    return out


LINES = 3 * 3 + 1
PLANES = 3 * 3 + 3 * 9 + 1


def greet(me, core, spot, planes):
    barrier = pltpu.get_barrier_semaphore()
    peers = [me + 1 - 2 * core]
    for g in range(3):
        near = plane_peers(me, spot, (g, (g + 1) % 3))
        peers += [d for d, (a, b), _ in near if a and (planes or not b)]
    for peer in peers:
        pl.semaphore_signal(barrier, inc=1, device_id=(peer,), device_id_type=MESH)
    return barrier


def send(src, dst, send_sem, recv_sem, device):
    copy = pltpu.make_async_remote_copy(
        src_ref=src,
        dst_ref=dst,
        send_sem=send_sem,
        recv_sem=recv_sem,
        device_id=(device,),
        device_id_type=MESH,
    )
    copy.start()
    return copy


def nothing():
    pass


def gather_stages(out, place_now, sems, beside, late=None):
    me, core, spot = place_now
    send_sem, recv_sem, core_send, core_recv = sems
    partner = me + 1 - 2 * core

    def where(stage, g, last):
        done = [(g + t) % 3 for t in range(stage)]
        spots = [slice(None) if a in done else spot[a] for a in range(3)]
        spots[(g + stage) % 3] = last
        return tuple(spots) + (core, g)

    def start(stage, g, rows, turn):
        axis = (g + stage) % 3
        part = out.at[where(stage, g, spot[axis]) + rows]
        return [
            send(
                part,
                part,
                send_sem.at[turn, g, step - 1],
                recv_sem.at[turn, g, 3 - step],
                peer_of(me, spot, axis, step),
            )
            for step in (1, 2, 3)
        ]

    if late is not None:
        copies = [start(0, g, (pl.ds(8, 8),), 0) for g in range(3)]
        late()
        copies = [copies[g] + start(0, g, (pl.ds(0, 8),), 3) for g in range(3)]
    else:
        copies = [start(0, g, (), 0) for g in range(3)]
    beside[0]()
    passed = []
    for stage in (1, 2):
        ahead = []
        for g in range(3):
            for copy in copies[g]:
                copy.wait()
            ahead.append(start(stage, g, (), stage))
            if stage == 2:
                part = out.at[where(stage, g, spot[(g + stage) % 3])]
                passed.append(send(part, part, core_send.at[g, 0], core_recv.at[g, 0], partner))
        copies = ahead
        beside[stage]()
    for k, step in enumerate((3, 1, 2)):
        for g in range(3):
            axis = (g + 2) % 3
            copies[g][step - 1].wait_recv()
            part = out.at[where(2, g, lax.rem(spot[axis] + SIDE - step, SIDE))]
            passed.append(send(part, part, core_send.at[g, 1 + k], core_recv.at[g, 1 + k], partner))
    for copy in copies[0] + copies[1] + copies[2]:
        copy.wait_send()
    for copy in passed:
        copy.wait()


def sum_stages(terms, place_now, buffers, sems):
    me, core, spot = place_now
    core_in, s1, r2, s2, r3 = buffers
    plane_send, plane_recv, line_send, line_recv, core_send, core_recv = sems
    swaps = []
    for g in range(3):
        part = terms.at[:, :, :, 1 - core, g]
        swaps.append(send(part, core_in.at[g], core_send.at[g], core_recv.at[g], me + 1 - 2 * core))
    copies = []
    for g in range(3):
        swaps[g].wait_recv()
        for a in range(SIDE):
            s1[g, a] = terms[a, :, :, core, g] + core_in[g, a]
        for step in (1, 2, 3):
            to = lax.rem(spot[g] + step, SIDE)
            copies.append(
                send(
                    s1.at[(g,) + (slice(None),) * g + (to,)],
                    r2.at[g, 3 - step],
                    line_send.at[g, step - 1],
                    line_recv.at[g, 3 - step],
                    peer_of(me, spot, g, step),
                )
            )
    spread = [[], [], []]
    left = [[a for a in range(3) if a != g] for g in range(3)]
    for g in range(3):
        for k in range(3):
            copies[3 * g + k].wait_recv()
        mine = (g,) + (slice(None),) * g + (spot[g],)
        s2[g] = (s1[mine] + r2[g, 0]) + (r2[g, 1] + r2[g, 2])
        for device, (a, b), there in plane_peers(me, spot, left[g]):
            to = (lax.rem(spot[left[g][0]] + a, SIDE), lax.rem(spot[left[g][1]] + b, SIDE))
            spread[g].append(
                send(
                    s2.at[(g,) + to],
                    r3.at[g, there],
                    plane_send.at[g, SIDE * a + b],
                    plane_recv.at[g, there],
                    device,
                )
            )
    totals = []
    for g in range(3):
        for copy in spread[g]:
            copy.wait_recv()
        terms_now = [s2[g, spot[left[g][0]], spot[left[g][1]]]] + [r3[g, k] for k in range(1, 16)]
        while len(terms_now) > 1:
            terms_now = [x + y for x, y in zip(terms_now[::2], terms_now[1::2])]
        totals.append(terms_now[0])
    for copy in swaps + copies + spread[0] + spread[1] + spread[2]:
        copy.wait_send()
    return totals


def sum_buffers(rows):
    tail = (rows, LANES)
    return [
        VMEM((3, 4, 4, 4) + tail, f32),
        VMEM((3, 4, 4, 4) + tail, f32),
        VMEM((3, 3, 4, 4) + tail, f32),
        VMEM((3, 4, 4) + tail, f32),
        VMEM((3, 16) + tail, f32),
    ]


def stage_sems(gather):
    dma = pltpu.SemaphoreType.DMA
    if gather:
        return [dma((4, 3, 3)), dma((4, 3, 3)), dma((3, 4)), dma((3, 4))]
    return [dma((3, 16)), dma((3, 16)), dma((3, 3)), dma((3, 3)), dma((3,)), dma((3,))]


def halves(x):
    high = x.astype(bf16)
    return high, (x - high.astype(f32)).astype(bf16)


def times_factor(values, high, low, contract):
    top, bottom = halves(values)
    both = jnp.concatenate([top, bottom], axis=0)
    dims = (((1,), (contract,)), ((), ()))
    first = lax.dot_general(both, high[...], dims, preferred_element_type=f32)
    second = lax.dot_general(both, low[...], dims, preferred_element_type=f32)
    return (first[:8] + first[8:]) + (second[:8] + second[8:])


def apply_inverse(values, high, low):
    return times_factor(times_factor(values, high, low, 1), high, low, 0)


def at_owner(ids):
    device = lax.shift_right_logical(ids[...], 9)
    return lax.broadcasted_iota(jnp.int32, (PATCHES, PN), 0) == device


def mark_local(ids, marks):
    local = lax.bitwise_and(ids[...], NODE_DEV - 1)
    found = lax.broadcasted_iota(jnp.int32, (NODE_DEV, PN), 0) == local
    marks[...] = jnp.where(found, 1.0, 0.0).astype(bf16)


def split_factor(factor, high, low):
    def step(t, _):
        part = pl.ds(pl.multiple_of(t * LANES, LANES), LANES)
        high[part, :], low[part, :] = halves(factor[part, :])
        return 0

    lax.fori_loop(0, PN // LANES, step, 0)


def factor_scratch():
    return [
        VMEM((PN, PN), f32),
        VMEM((PN, PN), bf16),
        VMEM((PN, PN), bf16),
        VMEM((NODE_DEV, PN), bf16),
        pltpu.SemaphoreType.DMA,
    ]


def patch_kernel(coords, disp, ids, factor_hbm, fluid_x, fluid_f, blend, names, *rest):
    table, fields, targets, nodes, factor, high, low, marks, factor_sem = rest[:9]
    node_sems, table_sems = rest[9:13], rest[13:17]
    me, core, spot = place()
    load = pltpu.make_async_copy(factor_hbm, factor, factor_sem)
    load.start()
    barrier = greet(me, core, spot, False)
    for g in range(3):
        for r in range(4):
            lanes = pl.ds(r * LANES, LANES)
            nodes[spot[0], spot[1], spot[2], core, g, pl.ds(r, 1), :] = coords[pl.ds(g, 1), lanes]
            nodes[spot[0], spot[1], spot[2], core, g, pl.ds(4 + r, 1), :] = disp[pl.ds(g, 1), lanes]
    mark_local(ids, marks)
    pl.semaphore_wait(barrier, LINES)

    def fill_fields():
        x, f, b = fluid_x[...], fluid_f[...], blend[...]
        square = GAIN * jnp.sum(x * x, axis=0, keepdims=True)
        share = b / jnp.sum(b, axis=0, keepdims=True)
        for c in range(3):
            fields[c] = x[c : c + 1]
            fields[3 + c] = f[c : c + 1]
        fields[6] = square
        for s in range(SLOTS):
            fields[7 + s] = share[s : s + 1]
            targets[s] = names[pl.ds(s, 1), :]

    def ready_factor():
        load.wait()
        split_factor(factor, high, low)

    gather_stages(nodes, (me, core, spot), node_sems, (fill_fields, ready_factor, nothing))

    rows = nodes.reshape(PATCHES * 24, LANES)

    def pick(h):
        pieces = []
        for g in range(3):
            first = 8 * g + 4 * h
            row = [rows[pl.ds(first + r, PATCHES, stride=24), :] for r in range(4)]
            pieces.append(jnp.concatenate(row, axis=1))
        top, bottom = halves(jnp.concatenate(pieces, axis=0))
        found = jnp.dot(top, marks[...], preferred_element_type=f32)
        found = found + jnp.dot(bottom, marks[...], preferred_element_type=f32)
        where = at_owner(ids)
        out = []
        for g in range(3):
            mine = jnp.where(where, found[g * PATCHES : (g + 1) * PATCHES], 0.0)
            out.append(jnp.sum(mine, axis=0, keepdims=True))
        return out

    moved = jnp.concatenate(pick(1) + [jnp.zeros((5, PN), f32)], axis=0)
    coeffs = apply_inverse(moved, high, low)

    def fill(values, first):
        for g in range(3):
            for s in range(8):
                lanes = slice(s * LANES, (s + 1) * LANES)
                table[spot[0], spot[1], spot[2], core, g, pl.ds(first + s, 1), :] = values[g][:, lanes]

    def fill_centres():
        fill([y * (-2.0 * GAIN) for y in pick(0)], 0)

    fill([coeffs[g : g + 1] for g in range(3)], 8)
    gather_stages(table, (me, core, spot), table_sems, (nothing,) * 3, fill_centres)


def patch_tables(node_coords, node_disp, node_list, factor, coords, loads, blend, names):
    points = coords.shape[1]
    vmem = pl.BlockSpec(memory_space=VMEM)
    return pl.pallas_call(
        patch_kernel,
        out_shape=(
            jax.ShapeDtypeStruct((4, 4, 4, 2, 3, 16, LANES), f32),
            jax.ShapeDtypeStruct((FIELDS, 1, points), f32),
            jax.ShapeDtypeStruct((SLOTS, 1, points), jnp.int32),
        ),
        in_specs=[vmem] * 3 + [pl.BlockSpec(memory_space=pl.ANY)] + [vmem] * 4,
        out_specs=[vmem] * 3,
        scratch_shapes=[VMEM((4, 4, 4, 2, 3, 8, LANES), f32)]
        + factor_scratch()
        + stage_sems(True)
        + stage_sems(True),
        compiler_params=pltpu.CompilerParams(
            collective_id=0, has_side_effects=True, vmem_limit_bytes=60 * 2**20
        ),
    )(node_coords, node_disp, node_list, factor, coords, loads, blend, names)


def load_kernel(terms_hbm, ids, factor_hbm, out, spread, factor, high, low, marks, factor_sem, terms, terms_sem, *rest):
    patch_buffers, node_buffers = rest[:5], rest[5:10]
    patch_sems, node_sems = rest[10:16], rest[16:22]
    me, core, spot = place()
    load = pltpu.make_async_copy(factor_hbm, factor, factor_sem)
    fill = pltpu.make_async_copy(terms_hbm, terms, terms_sem)
    fill.start()
    load.start()
    barrier = greet(me, core, spot, True)
    mark_local(ids, marks)
    load.wait()
    split_factor(factor, high, low)
    fill.wait()
    pl.semaphore_wait(barrier, PLANES)
    summed = sum_stages(terms, (me, core, spot), patch_buffers, patch_sems)
    rows = [jnp.concatenate([part[s : s + 1] for s in range(8)], axis=1) for part in summed]
    rows = jnp.concatenate(rows + [jnp.zeros((5, PN), f32)], axis=0)
    loads = apply_inverse(rows, high, low)
    where = at_owner(ids)
    parts = []
    for g in range(3):
        parts.extend(halves(jnp.where(where, loads[g : g + 1], 0.0)))
    found = lax.dot_general(
        jnp.concatenate(parts, axis=0),
        marks[...],
        (((1,), (1,)), ((), ())),
        preferred_element_type=f32,
    )
    flat = spread.reshape(PATCHES * 12, LANES)
    for g in range(3):
        base = 2 * g * PATCHES
        term = found[base : base + PATCHES] + found[base + PATCHES : base + 2 * PATCHES]
        for r in range(4):
            lanes = slice(r * LANES, (r + 1) * LANES)
            flat[pl.ds(4 * g + r, PATCHES, stride=12), :] = term[:, lanes]
    owned = sum_stages(spread, (me, core, spot), node_buffers, node_sems)
    for g in range(3):
        for r in range(4):
            out[pl.ds(g, 1), pl.ds(r * LANES, LANES)] = owned[g][r : r + 1]


def node_sums(terms, node_list, factor):
    vmem = pl.BlockSpec(memory_space=VMEM)
    hbm = pl.BlockSpec(memory_space=pl.ANY)
    return pl.pallas_call(
        load_kernel,
        out_shape=jax.ShapeDtypeStruct((3, NODE_DEV), f32),
        in_specs=[hbm, vmem, hbm],
        out_specs=vmem,
        scratch_shapes=[VMEM((4, 4, 4, 2, 3, 4, LANES), f32)]
        + factor_scratch()
        + [VMEM((4, 4, 4, 2, 3, 8, LANES), f32), pltpu.SemaphoreType.DMA]
        + sum_buffers(8)
        + sum_buffers(4)
        + stage_sems(False)
        + stage_sems(False),
        compiler_params=pltpu.CompilerParams(
            collective_id=1, has_side_effects=True, vmem_limit_bytes=60 * 2**20
        ),
    )(terms, node_list, factor)


FIELDS = 11
EARLY = 4


def fluid_kernel(*refs):
    patch, fields, table_hbm, disp, acc, work, table, table_sem, got = refs[:9]
    names, data = refs[9 : 9 + SLOTS], refs[9 + SLOTS :]
    fill = pltpu.make_async_copy(table_hbm, table, table_sem)
    fill.start()
    points = disp.shape[1]
    rows = [(patch.at[s], names[s]) for s in range(SLOTS)]
    rows += [(fields.at[j], data[j]) for j in range(FIELDS)]

    def scalars(k):
        first = EARLY * LANES
        where = (slice(None), pl.ds(first, points - first) if k else pl.ds(0, first))
        return [
            pltpu.make_async_copy(src.at[where], dst.at[where], got.at[k, j])
            for j, (src, dst) in enumerate(rows)
        ]

    for k in range(2):
        for copy in scalars(k):
            copy.start()
    lane = lax.broadcasted_iota(jnp.int32, (8, LANES), 1)

    def patch_step(p, _):
        y = [table[6 * p + 2 * c] for c in range(3)]
        total = (y[0] * y[0] + y[1] * y[1]) + y[2] * y[2]
        for c in range(3):
            work[p * 8 + c] = y[c]
            work[p * 8 + 4 + c] = table[6 * p + 2 * c + 1]
            acc[p * 3 + c] = jnp.zeros((8, LANES), f32)
        work[p * 8 + 3] = 1.0 + total * (1.0 / (4.0 * GAIN))
        return 0

    fill.wait()
    lax.fori_loop(0, PATCHES, patch_step, 0)

    for copy in scalars(0):
        copy.wait()

    def block_step(block, _):
        start = block * LANES

        @pl.when(block == EARLY)
        def _():
            for copy in scalars(1):
                copy.wait()

        def point_step(group, held):
            first = group * 128
            ahead = lane - first
            held = list(held)
            for q in range(128):
                i = start + first + q
                x, y, z, square = data[0][0, i], data[1][0, i], data[2][0, i], data[6][0, i]
                ps = [names[s][0, i] for s in range(SLOTS)]
                term = []
                for s in range(SLOTS):
                    p = ps[s] * 8
                    near = (work[p] * x + work[p + 1] * y) + (work[p + 2] * z + (work[p + 3] + square))
                    term.append(lax.rsqrt(near) * data[7 + s][0, i])
                old = [[acc[p * 3 + c] for c in range(3)] for p in ps]
                here = ahead == q
                for c in range(3):
                    dots = [work[ps[s] * 8 + 4 + c] * term[s] for s in range(SLOTS)]
                    value = (dots[0] + dots[1]) + (dots[2] + dots[3])
                    held[c] = jnp.where(here, jnp.sum(value, axis=1, keepdims=True), held[c])
                force = [data[3 + c][0, i] for c in range(3)]
                for s in range(SLOTS):
                    for c in range(3):
                        acc[ps[s] * 3 + c] = old[s][c] + term[s] * force[c]
            return tuple(held)

        held = lax.fori_loop(0, LANES // 128, point_step, (jnp.zeros((8, LANES), f32),) * 3)
        for c in range(3):
            total = jnp.sum(held[c], axis=0, keepdims=True)
            disp[pl.ds(c, 1), pl.ds(pl.multiple_of(start, LANES), LANES)] = total * (1.0 / 32.0)
        return 0

    lax.fori_loop(0, points // LANES, block_step, 0)


def fluid(patch, fields, table):
    points = fields.shape[2]
    return pl.pallas_call(
        fluid_kernel,
        out_shape=(
            jax.ShapeDtypeStruct((3, points), f32),
            jax.ShapeDtypeStruct((PATCHES * 3, 8, LANES), f32),
        ),
        in_specs=[pl.BlockSpec(memory_space=pl.ANY)] * 3,
        out_specs=[pl.BlockSpec(memory_space=VMEM)] * 2,
        scratch_shapes=[
            VMEM((PATCHES * 8, 8, LANES), f32),
            VMEM((PATCHES * 6, 8, LANES), f32),
            pltpu.SemaphoreType.DMA,
            pltpu.SemaphoreType.DMA((2, SLOTS + FIELDS)),
        ]
        + [pltpu.SMEM((1, points), jnp.int32)] * SLOTS
        + [pltpu.SMEM((1, points), f32)] * FIELDS,
    )(patch, fields, table)


def local(node_coords, node_disp, node_list, factor, fluid_coords, fluid_loads, fluid_patch, blend_raw):
    table, fields, names = patch_tables(
        node_coords,
        node_disp,
        node_list,
        factor[0],
        fluid_coords,
        fluid_loads,
        blend_raw.T,
        fluid_patch.T,
    )
    fluid_disp, terms = fluid(names, fields, table.reshape(PATCHES * 6, 8, LANES))
    node_loads = node_sums(terms.reshape(4, 4, 4, 2, 3, 8, LANES), node_list, factor[0])
    return fluid_disp, node_loads * (1.0 / 32.0)


def solution(mesh):
    placed = (
        P(None, "dev"),
        P(None, "dev"),
        P("dev", None),
        P("dev", None, None),
        P(None, "dev"),
        P(None, "dev"),
        P("dev", None),
        P("dev", None),
    )
    return jax.shard_map(
        local,
        mesh=mesh,
        in_specs=placed,
        out_specs=(P(None, "dev"), P(None, "dev")),
        check_vma=False,
    )
```

```python
import jax
import jax.numpy as jnp
from jax import lax
from jax.experimental import pallas as pl
from jax.experimental.pallas import tpu as pltpu
from jax.sharding import PartitionSpec as P

PN = 1024
SLOTS = 4
PATCHES = 128
NODE_DEV = 512
LANES = 128
SIDE = 4
STRIDE = (32, 8, 2)
GAIN = 8.0

f32 = jnp.float32
bf16 = jnp.bfloat16
VMEM = pltpu.VMEM
MESH = pl.DeviceIdType.MESH


def place():
    me = lax.axis_index("dev")
    return me, lax.rem(me, 2), tuple(lax.rem(me // s, SIDE) for s in STRIDE)


def peer_of(me, spot, axis, step):
    return me + (lax.rem(spot[axis] + step, SIDE) - spot[axis]) * STRIDE[axis]


def plane_peers(me, spot, axes):
    steps = [(a, b) for a in range(SIDE) for b in range(SIDE) if a or b]
    steps.sort(key=lambda ab: min(ab[0], SIDE - ab[0]) + min(ab[1], SIDE - ab[1]))
    out = []
    for a, b in steps:
        device = peer_of(peer_of(me, spot, axes[0], a), spot, axes[1], b)
        out.append((device, (a, b), ((SIDE - a) % SIDE) * SIDE + (SIDE - b) % SIDE))
    return out


LINES = 3 * 3 + 1
PLANES = 3 * 3 + 3 * 9 + 1


def greet(me, core, spot, planes):
    barrier = pltpu.get_barrier_semaphore()
    peers = [me + 1 - 2 * core]
    for g in range(3):
        near = plane_peers(me, spot, (g, (g + 1) % 3))
        peers += [d for d, (a, b), _ in near if a and (planes or not b)]
    for peer in peers:
        pl.semaphore_signal(barrier, inc=1, device_id=(peer,), device_id_type=MESH)
    return barrier


def send(src, dst, send_sem, recv_sem, device):
    copy = pltpu.make_async_remote_copy(
        src_ref=src,
        dst_ref=dst,
        send_sem=send_sem,
        recv_sem=recv_sem,
        device_id=(device,),
        device_id_type=MESH,
    )
    copy.start()
    return copy


def nothing():
    pass


def gather_stages(out, place_now, sems, beside, late=None):
    me, core, spot = place_now
    send_sem, recv_sem, core_send, core_recv = sems
    partner = me + 1 - 2 * core

    def where(stage, g, last):
        done = [(g + t) % 3 for t in range(stage)]
        spots = [slice(None) if a in done else spot[a] for a in range(3)]
        spots[(g + stage) % 3] = last
        return tuple(spots) + (core, g)

    def start(stage, g, rows, turn):
        axis = (g + stage) % 3
        part = out.at[where(stage, g, spot[axis]) + rows]
        return [
            send(
                part,
                part,
                send_sem.at[turn, g, step - 1],
                recv_sem.at[turn, g, 3 - step],
                peer_of(me, spot, axis, step),
            )
            for step in (1, 2, 3)
        ]

    if late is not None:
        copies = [start(0, g, (pl.ds(8, 8),), 0) for g in range(3)]
        late()
        copies = [copies[g] + start(0, g, (pl.ds(0, 8),), 3) for g in range(3)]
    else:
        copies = [start(0, g, (), 0) for g in range(3)]
    beside[0]()
    passed = []
    for stage in (1, 2):
        ahead = []
        for g in range(3):
            for copy in copies[g]:
                copy.wait()
            ahead.append(start(stage, g, (), stage))
            if stage == 2:
                part = out.at[where(stage, g, spot[(g + stage) % 3])]
                passed.append(send(part, part, core_send.at[g, 0], core_recv.at[g, 0], partner))
        copies = ahead
        beside[stage]()
    for k, step in enumerate((3, 1, 2)):
        for g in range(3):
            axis = (g + 2) % 3
            copies[g][step - 1].wait_recv()
            part = out.at[where(2, g, lax.rem(spot[axis] + SIDE - step, SIDE))]
            passed.append(send(part, part, core_send.at[g, 1 + k], core_recv.at[g, 1 + k], partner))
    for copy in copies[0] + copies[1] + copies[2]:
        copy.wait_send()
    for copy in passed:
        copy.wait()


def sum_stages(terms, place_now, buffers, sems):
    me, core, spot = place_now
    core_in, s1, r2, s2, r3 = buffers
    plane_send, plane_recv, line_send, line_recv, core_send, core_recv = sems
    swaps = []
    for g in range(3):
        part = terms.at[:, :, :, 1 - core, g]
        swaps.append(send(part, core_in.at[g], core_send.at[g], core_recv.at[g], me + 1 - 2 * core))
    copies = []
    for g in range(3):
        swaps[g].wait_recv()
        for a in range(SIDE):
            s1[g, a] = terms[a, :, :, core, g] + core_in[g, a]
        for step in (1, 2, 3):
            to = lax.rem(spot[g] + step, SIDE)
            copies.append(
                send(
                    s1.at[(g,) + (slice(None),) * g + (to,)],
                    r2.at[g, 3 - step],
                    line_send.at[g, step - 1],
                    line_recv.at[g, 3 - step],
                    peer_of(me, spot, g, step),
                )
            )
    spread = [[], [], []]
    left = [[a for a in range(3) if a != g] for g in range(3)]
    for g in range(3):
        for k in range(3):
            copies[3 * g + k].wait_recv()
        mine = (g,) + (slice(None),) * g + (spot[g],)
        s2[g] = (s1[mine] + r2[g, 0]) + (r2[g, 1] + r2[g, 2])
        for device, (a, b), there in plane_peers(me, spot, left[g]):
            to = (lax.rem(spot[left[g][0]] + a, SIDE), lax.rem(spot[left[g][1]] + b, SIDE))
            spread[g].append(
                send(
                    s2.at[(g,) + to],
                    r3.at[g, there],
                    plane_send.at[g, SIDE * a + b],
                    plane_recv.at[g, there],
                    device,
                )
            )
    totals = []
    for g in range(3):
        for copy in spread[g]:
            copy.wait_recv()
        terms_now = [s2[g, spot[left[g][0]], spot[left[g][1]]]] + [r3[g, k] for k in range(1, 16)]
        while len(terms_now) > 1:
            terms_now = [x + y for x, y in zip(terms_now[::2], terms_now[1::2])]
        totals.append(terms_now[0])
    for copy in swaps + copies + spread[0] + spread[1] + spread[2]:
        copy.wait_send()
    return totals


def sum_buffers(rows):
    tail = (rows, LANES)
    return [
        VMEM((3, 4, 4, 4) + tail, f32),
        VMEM((3, 4, 4, 4) + tail, f32),
        VMEM((3, 3, 4, 4) + tail, f32),
        VMEM((3, 4, 4) + tail, f32),
        VMEM((3, 16) + tail, f32),
    ]


def stage_sems(gather):
    dma = pltpu.SemaphoreType.DMA
    if gather:
        return [dma((4, 3, 3)), dma((4, 3, 3)), dma((3, 4)), dma((3, 4))]
    return [dma((3, 16)), dma((3, 16)), dma((3, 3)), dma((3, 3)), dma((3,)), dma((3,))]


def halves(x):
    high = x.astype(bf16)
    return high, (x - high.astype(f32)).astype(bf16)


def times_factor(values, high, low, contract):
    top, bottom = halves(values)
    both = jnp.concatenate([top, bottom], axis=0)
    dims = (((1,), (contract,)), ((), ()))
    first = lax.dot_general(both, high[...], dims, preferred_element_type=f32)
    second = lax.dot_general(both, low[...], dims, preferred_element_type=f32)
    return (first[:8] + first[8:]) + (second[:8] + second[8:])


def apply_inverse(values, high, low):
    return times_factor(times_factor(values, high, low, 1), high, low, 0)


def at_owner(ids):
    device = lax.shift_right_logical(ids[...], 9)
    return lax.broadcasted_iota(jnp.int32, (PATCHES, PN), 0) == device


def mark_local(ids, marks):
    local = lax.bitwise_and(ids[...], NODE_DEV - 1)
    found = lax.broadcasted_iota(jnp.int32, (NODE_DEV, PN), 0) == local
    marks[...] = jnp.where(found, 1.0, 0.0).astype(bf16)


def split_factor(factor, high, low):
    def step(t, _):
        part = pl.ds(pl.multiple_of(t * LANES, LANES), LANES)
        high[part, :], low[part, :] = halves(factor[part, :])
        return 0

    lax.fori_loop(0, PN // LANES, step, 0)


def factor_scratch():
    return [
        VMEM((PN, PN), f32),
        VMEM((PN, PN), bf16),
        VMEM((PN, PN), bf16),
        VMEM((NODE_DEV, PN), bf16),
        pltpu.SemaphoreType.DMA,
    ]


def patch_kernel(coords, disp, ids, factor_hbm, fluid_x, fluid_f, blend, names, *rest):
    table, fields, targets, nodes, factor, high, low, marks, factor_sem = rest[:9]
    node_sems, table_sems = rest[9:13], rest[13:17]
    me, core, spot = place()
    load = pltpu.make_async_copy(factor_hbm, factor, factor_sem)
    load.start()
    barrier = greet(me, core, spot, False)
    for g in range(3):
        for r in range(4):
            lanes = pl.ds(r * LANES, LANES)
            nodes[spot[0], spot[1], spot[2], core, g, pl.ds(r, 1), :] = coords[pl.ds(g, 1), lanes]
            nodes[spot[0], spot[1], spot[2], core, g, pl.ds(4 + r, 1), :] = disp[pl.ds(g, 1), lanes]
    mark_local(ids, marks)
    pl.semaphore_wait(barrier, LINES)

    def fill_fields():
        x, f, b = fluid_x[...], fluid_f[...], blend[...]
        square = GAIN * jnp.sum(x * x, axis=0, keepdims=True)
        share = b / jnp.sum(b, axis=0, keepdims=True)
        for c in range(3):
            fields[c] = x[c : c + 1]
            fields[3 + c] = f[c : c + 1]
        fields[6] = square
        for s in range(SLOTS):
            fields[7 + s] = share[s : s + 1]
            targets[s] = names[pl.ds(s, 1), :]

    def ready_factor():
        load.wait()
        split_factor(factor, high, low)

    gather_stages(nodes, (me, core, spot), node_sems, (fill_fields, ready_factor, nothing))

    rows = nodes.reshape(PATCHES * 24, LANES)

    def pick(h):
        pieces = []
        for g in range(3):
            first = 8 * g + 4 * h
            row = [rows[pl.ds(first + r, PATCHES, stride=24), :] for r in range(4)]
            pieces.append(jnp.concatenate(row, axis=1))
        top, bottom = halves(jnp.concatenate(pieces, axis=0))
        found = jnp.dot(top, marks[...], preferred_element_type=f32)
        found = found + jnp.dot(bottom, marks[...], preferred_element_type=f32)
        where = at_owner(ids)
        out = []
        for g in range(3):
            mine = jnp.where(where, found[g * PATCHES : (g + 1) * PATCHES], 0.0)
            out.append(jnp.sum(mine, axis=0, keepdims=True))
        return out

    moved = jnp.concatenate(pick(1) + [jnp.zeros((5, PN), f32)], axis=0)
    coeffs = apply_inverse(moved, high, low)

    def fill(values, first):
        for g in range(3):
            for s in range(8):
                lanes = slice(s * LANES, (s + 1) * LANES)
                table[spot[0], spot[1], spot[2], core, g, pl.ds(first + s, 1), :] = values[g][:, lanes]

    def fill_centres():
        fill([y * (-2.0 * GAIN) for y in pick(0)], 0)

    fill([coeffs[g : g + 1] for g in range(3)], 8)
    gather_stages(table, (me, core, spot), table_sems, (nothing,) * 3, fill_centres)


def patch_tables(node_coords, node_disp, node_list, factor, coords, loads, blend, names):
    points = coords.shape[1]
    vmem = pl.BlockSpec(memory_space=VMEM)
    return pl.pallas_call(
        patch_kernel,
        out_shape=(
            jax.ShapeDtypeStruct((4, 4, 4, 2, 3, 16, LANES), f32),
            jax.ShapeDtypeStruct((FIELDS, 1, points), f32),
            jax.ShapeDtypeStruct((SLOTS, 1, points), jnp.int32),
        ),
        in_specs=[vmem] * 3 + [pl.BlockSpec(memory_space=pl.ANY)] + [vmem] * 4,
        out_specs=[vmem] * 3,
        scratch_shapes=[VMEM((4, 4, 4, 2, 3, 8, LANES), f32)]
        + factor_scratch()
        + stage_sems(True)
        + stage_sems(True),
        compiler_params=pltpu.CompilerParams(
            collective_id=0, has_side_effects=True, vmem_limit_bytes=60 * 2**20
        ),
    )(node_coords, node_disp, node_list, factor, coords, loads, blend, names)


def load_kernel(terms_hbm, ids, factor_hbm, out, spread, factor, high, low, marks, factor_sem, terms, terms_sem, *rest):
    patch_buffers, node_buffers = rest[:5], rest[5:10]
    patch_sems, node_sems = rest[10:16], rest[16:22]
    me, core, spot = place()
    load = pltpu.make_async_copy(factor_hbm, factor, factor_sem)
    fill = pltpu.make_async_copy(terms_hbm, terms, terms_sem)
    fill.start()
    load.start()
    barrier = greet(me, core, spot, True)
    mark_local(ids, marks)
    load.wait()
    split_factor(factor, high, low)
    fill.wait()
    pl.semaphore_wait(barrier, PLANES)
    summed = sum_stages(terms, (me, core, spot), patch_buffers, patch_sems)
    rows = [jnp.concatenate([part[s : s + 1] for s in range(8)], axis=1) for part in summed]
    rows = jnp.concatenate(rows + [jnp.zeros((5, PN), f32)], axis=0)
    loads = apply_inverse(rows, high, low)
    where = at_owner(ids)
    parts = []
    for g in range(3):
        parts.extend(halves(jnp.where(where, loads[g : g + 1], 0.0)))
    found = lax.dot_general(
        jnp.concatenate(parts, axis=0),
        marks[...],
        (((1,), (1,)), ((), ())),
        preferred_element_type=f32,
    )
    flat = spread.reshape(PATCHES * 12, LANES)
    for g in range(3):
        base = 2 * g * PATCHES
        term = found[base : base + PATCHES] + found[base + PATCHES : base + 2 * PATCHES]
        for r in range(4):
            lanes = slice(r * LANES, (r + 1) * LANES)
            flat[pl.ds(4 * g + r, PATCHES, stride=12), :] = term[:, lanes]
    owned = sum_stages(spread, (me, core, spot), node_buffers, node_sems)
    for g in range(3):
        for r in range(4):
            out[pl.ds(g, 1), pl.ds(r * LANES, LANES)] = owned[g][r : r + 1]


def node_sums(terms, node_list, factor):
    vmem = pl.BlockSpec(memory_space=VMEM)
    hbm = pl.BlockSpec(memory_space=pl.ANY)
    return pl.pallas_call(
        load_kernel,
        out_shape=jax.ShapeDtypeStruct((3, NODE_DEV), f32),
        in_specs=[hbm, vmem, hbm],
        out_specs=vmem,
        scratch_shapes=[VMEM((4, 4, 4, 2, 3, 4, LANES), f32)]
        + factor_scratch()
        + [VMEM((4, 4, 4, 2, 3, 8, LANES), f32), pltpu.SemaphoreType.DMA]
        + sum_buffers(8)
        + sum_buffers(4)
        + stage_sems(False)
        + stage_sems(False),
        compiler_params=pltpu.CompilerParams(
            collective_id=1, has_side_effects=True, vmem_limit_bytes=60 * 2**20
        ),
    )(terms, node_list, factor)


FIELDS = 11
EARLY = 4


def fluid_kernel(*refs):
    patch, fields, table_hbm, disp, acc, work, table, held, table_sem, got = refs[:10]
    names, data = refs[10 : 10 + SLOTS], refs[10 + SLOTS :]
    fill = pltpu.make_async_copy(table_hbm, table, table_sem)
    fill.start()
    points = disp.shape[1]
    rows = [(patch.at[s], names[s]) for s in range(SLOTS)]
    rows += [(fields.at[j], data[j]) for j in range(FIELDS)]

    def scalars(k):
        first = EARLY * LANES
        where = (slice(None), pl.ds(first, points - first) if k else pl.ds(0, first))
        return [
            pltpu.make_async_copy(src.at[where], dst.at[where], got.at[k, j])
            for j, (src, dst) in enumerate(rows)
        ]

    for k in range(2):
        for copy in scalars(k):
            copy.start()
    def patch_step(p, _):
        y = [table[6 * p + 2 * c] for c in range(3)]
        total = (y[0] * y[0] + y[1] * y[1]) + y[2] * y[2]
        for c in range(3):
            work[p * 8 + c] = y[c]
            work[p * 8 + 4 + c] = table[6 * p + 2 * c + 1]
            acc[p * 3 + c] = jnp.zeros((8, LANES), f32)
        work[p * 8 + 3] = 1.0 + total * (1.0 / (4.0 * GAIN))
        return 0

    fill.wait()
    lax.fori_loop(0, PATCHES, patch_step, 0)

    for copy in scalars(0):
        copy.wait()

    def block_step(block, _):
        start = block * LANES

        @pl.when(block == EARLY)
        def _():
            for copy in scalars(1):
                copy.wait()

        for q in range(LANES):
            i = start + q
            x, y, z, square = data[0][0, i], data[1][0, i], data[2][0, i], data[6][0, i]
            ps = [names[s][0, i] for s in range(SLOTS)]
            term = []
            for s in range(SLOTS):
                p = ps[s] * 8
                near = (work[p] * x + work[p + 1] * y) + (work[p + 2] * z + (work[p + 3] + square))
                term.append(lax.rsqrt(near) * data[7 + s][0, i])
            old = [[acc[p * 3 + c] for c in range(3)] for p in ps]
            for c in range(3):
                dots = [work[ps[s] * 8 + 4 + c] * term[s] for s in range(SLOTS)]
                value = (dots[0] + dots[1]) + (dots[2] + dots[3])
                held[c, :, pl.ds(q, 1)] = jnp.sum(value, axis=1, keepdims=True)
            force = [data[3 + c][0, i] for c in range(3)]
            for s in range(SLOTS):
                for c in range(3):
                    acc[ps[s] * 3 + c] = old[s][c] + term[s] * force[c]
        for c in range(3):
            total = jnp.sum(held[c], axis=0, keepdims=True)
            disp[pl.ds(c, 1), pl.ds(pl.multiple_of(start, LANES), LANES)] = total * (1.0 / 32.0)
        return 0

    lax.fori_loop(0, points // LANES, block_step, 0)


def fluid(patch, fields, table):
    points = fields.shape[2]
    return pl.pallas_call(
        fluid_kernel,
        out_shape=(
            jax.ShapeDtypeStruct((3, points), f32),
            jax.ShapeDtypeStruct((PATCHES * 3, 8, LANES), f32),
        ),
        in_specs=[pl.BlockSpec(memory_space=pl.ANY)] * 3,
        out_specs=[pl.BlockSpec(memory_space=VMEM)] * 2,
        scratch_shapes=[
            VMEM((PATCHES * 8, 8, LANES), f32),
            VMEM((PATCHES * 6, 8, LANES), f32),
            VMEM((3, 8, LANES), f32),
            pltpu.SemaphoreType.DMA,
            pltpu.SemaphoreType.DMA((2, SLOTS + FIELDS)),
        ]
        + [pltpu.SMEM((1, points), jnp.int32)] * SLOTS
        + [pltpu.SMEM((1, points), f32)] * FIELDS,
    )(patch, fields, table)


def local(node_coords, node_disp, node_list, factor, fluid_coords, fluid_loads, fluid_patch, blend_raw):
    table, fields, names = patch_tables(
        node_coords,
        node_disp,
        node_list,
        factor[0],
        fluid_coords,
        fluid_loads,
        blend_raw.T,
        fluid_patch.T,
    )
    fluid_disp, terms = fluid(names, fields, table.reshape(PATCHES * 6, 8, LANES))
    node_loads = node_sums(terms.reshape(4, 4, 4, 2, 3, 8, LANES), node_list, factor[0])
    return fluid_disp, node_loads * (1.0 / 32.0)


def solution(mesh):
    placed = (
        P(None, "dev"),
        P(None, "dev"),
        P("dev", None),
        P("dev", None, None),
        P(None, "dev"),
        P(None, "dev"),
        P("dev", None),
        P("dev", None),
    )
    return jax.shard_map(
        local,
        mesh=mesh,
        in_specs=placed,
        out_specs=(P(None, "dev"), P(None, "dev")),
        check_vma=False,
    )
```

```python
import jax
import jax.numpy as jnp
from jax import lax
from jax.experimental import pallas as pl
from jax.experimental.pallas import tpu as pltpu
from jax.sharding import PartitionSpec as P

PN = 1024
SLOTS = 4
PATCHES = 128
NODE_DEV = 512
LANES = 128
SIDE = 4
STRIDE = (32, 8, 2)
GAIN = 8.0

f32 = jnp.float32
bf16 = jnp.bfloat16
VMEM = pltpu.VMEM
MESH = pl.DeviceIdType.MESH


def place():
    me = lax.axis_index("dev")
    return me, lax.rem(me, 2), tuple(lax.rem(me // s, SIDE) for s in STRIDE)


def peer_of(me, spot, axis, step):
    return me + (lax.rem(spot[axis] + step, SIDE) - spot[axis]) * STRIDE[axis]


def plane_peers(me, spot, axes):
    steps = [(a, b) for a in range(SIDE) for b in range(SIDE) if a or b]
    steps.sort(key=lambda ab: min(ab[0], SIDE - ab[0]) + min(ab[1], SIDE - ab[1]))
    out = []
    for a, b in steps:
        device = peer_of(peer_of(me, spot, axes[0], a), spot, axes[1], b)
        out.append((device, (a, b), ((SIDE - a) % SIDE) * SIDE + (SIDE - b) % SIDE))
    return out


LINES = 3 * 3 + 1
PLANES = 3 * 3 + 3 * 9 + 1


def greet(me, core, spot, planes):
    barrier = pltpu.get_barrier_semaphore()
    peers = [me + 1 - 2 * core]
    for g in range(3):
        near = plane_peers(me, spot, (g, (g + 1) % 3))
        peers += [d for d, (a, b), _ in near if a and (planes or not b)]
    for peer in peers:
        pl.semaphore_signal(barrier, inc=1, device_id=(peer,), device_id_type=MESH)
    return barrier


def send(src, dst, send_sem, recv_sem, device):
    copy = pltpu.make_async_remote_copy(
        src_ref=src,
        dst_ref=dst,
        send_sem=send_sem,
        recv_sem=recv_sem,
        device_id=(device,),
        device_id_type=MESH,
    )
    copy.start()
    return copy


def nothing():
    pass


def gather_stages(out, place_now, sems, beside, late=None):
    me, core, spot = place_now
    send_sem, recv_sem, core_send, core_recv = sems
    partner = me + 1 - 2 * core

    def where(stage, g, last):
        done = [(g + t) % 3 for t in range(stage)]
        spots = [slice(None) if a in done else spot[a] for a in range(3)]
        spots[(g + stage) % 3] = last
        return tuple(spots) + (core, g)

    def start(stage, g, rows, turn):
        axis = (g + stage) % 3
        part = out.at[where(stage, g, spot[axis]) + rows]
        return [
            send(
                part,
                part,
                send_sem.at[turn, g, step - 1],
                recv_sem.at[turn, g, 3 - step],
                peer_of(me, spot, axis, step),
            )
            for step in (1, 2, 3)
        ]

    if late is not None:
        copies = [start(0, g, (pl.ds(8, 8),), 0) for g in range(3)]
        late()
        copies = [copies[g] + start(0, g, (pl.ds(0, 8),), 3) for g in range(3)]
    else:
        copies = [start(0, g, (), 0) for g in range(3)]
    beside[0]()
    passed = []
    for stage in (1, 2):
        ahead = []
        for g in range(3):
            for copy in copies[g]:
                copy.wait()
            ahead.append(start(stage, g, (), stage))
            if stage == 2:
                part = out.at[where(stage, g, spot[(g + stage) % 3])]
                passed.append(send(part, part, core_send.at[g, 0], core_recv.at[g, 0], partner))
        copies = ahead
        beside[stage]()
    for k, step in enumerate((3, 1, 2)):
        for g in range(3):
            axis = (g + 2) % 3
            copies[g][step - 1].wait_recv()
            part = out.at[where(2, g, lax.rem(spot[axis] + SIDE - step, SIDE))]
            passed.append(send(part, part, core_send.at[g, 1 + k], core_recv.at[g, 1 + k], partner))
    for copy in copies[0] + copies[1] + copies[2]:
        copy.wait_send()
    for copy in passed:
        copy.wait()


def sum_stages(terms, place_now, buffers, sems, beside):
    me, core, spot = place_now
    core_in, s1, r2, s2, r3 = buffers
    plane_send, plane_recv, line_send, line_recv, core_send, core_recv = sems
    swaps = []
    for g in range(3):
        part = terms.at[:, :, :, 1 - core, g]
        swaps.append(send(part, core_in.at[g], core_send.at[g], core_recv.at[g], me + 1 - 2 * core))
    copies = []
    for g in range(3):
        swaps[g].wait_recv()
        for a in range(SIDE):
            s1[g, a] = terms[a, :, :, core, g] + core_in[g, a]
        for step in (1, 2, 3):
            to = lax.rem(spot[g] + step, SIDE)
            copies.append(
                send(
                    s1.at[(g,) + (slice(None),) * g + (to,)],
                    r2.at[g, 3 - step],
                    line_send.at[g, step - 1],
                    line_recv.at[g, 3 - step],
                    peer_of(me, spot, g, step),
                )
            )
    beside()
    spread = [[], [], []]
    left = [[a for a in range(3) if a != g] for g in range(3)]
    for g in range(3):
        for k in range(3):
            copies[3 * g + k].wait_recv()
        mine = (g,) + (slice(None),) * g + (spot[g],)
        s2[g] = (s1[mine] + r2[g, 0]) + (r2[g, 1] + r2[g, 2])
        for device, (a, b), there in plane_peers(me, spot, left[g]):
            to = (lax.rem(spot[left[g][0]] + a, SIDE), lax.rem(spot[left[g][1]] + b, SIDE))
            spread[g].append(
                send(
                    s2.at[(g,) + to],
                    r3.at[g, there],
                    plane_send.at[g, SIDE * a + b],
                    plane_recv.at[g, there],
                    device,
                )
            )
    totals = []
    for g in range(3):
        for copy in spread[g]:
            copy.wait_recv()
        terms_now = [s2[g, spot[left[g][0]], spot[left[g][1]]]] + [r3[g, k] for k in range(1, 16)]
        while len(terms_now) > 1:
            terms_now = [x + y for x, y in zip(terms_now[::2], terms_now[1::2])]
        totals.append(terms_now[0])
    for copy in swaps + copies + spread[0] + spread[1] + spread[2]:
        copy.wait_send()
    return totals


def sum_buffers(rows):
    tail = (rows, LANES)
    return [
        VMEM((3, 4, 4, 4) + tail, f32),
        VMEM((3, 4, 4, 4) + tail, f32),
        VMEM((3, 3, 4, 4) + tail, f32),
        VMEM((3, 4, 4) + tail, f32),
        VMEM((3, 16) + tail, f32),
    ]


def stage_sems(gather):
    dma = pltpu.SemaphoreType.DMA
    if gather:
        return [dma((4, 3, 3)), dma((4, 3, 3)), dma((3, 4)), dma((3, 4))]
    return [dma((3, 16)), dma((3, 16)), dma((3, 3)), dma((3, 3)), dma((3,)), dma((3,))]


def halves(x):
    high = x.astype(bf16)
    return high, (x - high.astype(f32)).astype(bf16)


def times_factor(values, high, low, contract):
    top, bottom = halves(values)
    both = jnp.concatenate([top, bottom], axis=0)
    dims = (((1,), (contract,)), ((), ()))
    first = lax.dot_general(both, high[...], dims, preferred_element_type=f32)
    second = lax.dot_general(both, low[...], dims, preferred_element_type=f32)
    return (first[:8] + first[8:]) + (second[:8] + second[8:])


def apply_inverse(values, high, low):
    return times_factor(times_factor(values, high, low, 1), high, low, 0)


def at_owner(ids):
    device = lax.shift_right_logical(ids[...], 9)
    return lax.broadcasted_iota(jnp.int32, (PATCHES, PN), 0) == device


def mark_local(ids, marks):
    local = lax.bitwise_and(ids[...], NODE_DEV - 1)
    found = lax.broadcasted_iota(jnp.int32, (NODE_DEV, PN), 0) == local
    marks[...] = jnp.where(found, 1.0, 0.0).astype(bf16)


def split_factor(factor, high, low):
    def step(t, _):
        part = pl.ds(pl.multiple_of(t * LANES, LANES), LANES)
        high[part, :], low[part, :] = halves(factor[part, :])
        return 0

    lax.fori_loop(0, PN // LANES, step, 0)


def factor_scratch():
    return [
        VMEM((PN, PN), f32),
        VMEM((PN, PN), bf16),
        VMEM((PN, PN), bf16),
        VMEM((NODE_DEV, PN), bf16),
        pltpu.SemaphoreType.DMA,
    ]


def patch_kernel(coords, disp, ids, factor_hbm, fluid_x, fluid_f, blend, names, *rest):
    table, fields, targets, nodes, factor, high, low, marks, factor_sem = rest[:9]
    node_sems, table_sems = rest[9:13], rest[13:17]
    me, core, spot = place()
    load = pltpu.make_async_copy(factor_hbm, factor, factor_sem)
    load.start()
    barrier = greet(me, core, spot, False)
    for g in range(3):
        for r in range(4):
            lanes = pl.ds(r * LANES, LANES)
            nodes[spot[0], spot[1], spot[2], core, g, pl.ds(r, 1), :] = coords[pl.ds(g, 1), lanes]
            nodes[spot[0], spot[1], spot[2], core, g, pl.ds(4 + r, 1), :] = disp[pl.ds(g, 1), lanes]
    mark_local(ids, marks)
    pl.semaphore_wait(barrier, LINES)

    def fill_fields():
        x, f, b = fluid_x[...], fluid_f[...], blend[...]
        square = GAIN * jnp.sum(x * x, axis=0, keepdims=True)
        share = b / jnp.sum(b, axis=0, keepdims=True)
        for c in range(3):
            fields[c] = x[c : c + 1]
            fields[3 + c] = f[c : c + 1]
        fields[6] = square
        for s in range(SLOTS):
            fields[7 + s] = share[s : s + 1]
            targets[s] = names[pl.ds(s, 1), :]

    def ready_factor():
        load.wait()
        split_factor(factor, high, low)

    gather_stages(nodes, (me, core, spot), node_sems, (fill_fields, ready_factor, nothing))

    rows = nodes.reshape(PATCHES * 24, LANES)

    def pick(h):
        pieces = []
        for g in range(3):
            first = 8 * g + 4 * h
            row = [rows[pl.ds(first + r, PATCHES, stride=24), :] for r in range(4)]
            pieces.append(jnp.concatenate(row, axis=1))
        top, bottom = halves(jnp.concatenate(pieces, axis=0))
        found = jnp.dot(top, marks[...], preferred_element_type=f32)
        found = found + jnp.dot(bottom, marks[...], preferred_element_type=f32)
        where = at_owner(ids)
        out = []
        for g in range(3):
            mine = jnp.where(where, found[g * PATCHES : (g + 1) * PATCHES], 0.0)
            out.append(jnp.sum(mine, axis=0, keepdims=True))
        return out

    moved = jnp.concatenate(pick(1) + [jnp.zeros((5, PN), f32)], axis=0)
    coeffs = apply_inverse(moved, high, low)

    def fill(values, first):
        for g in range(3):
            for s in range(8):
                lanes = slice(s * LANES, (s + 1) * LANES)
                table[spot[0], spot[1], spot[2], core, g, pl.ds(first + s, 1), :] = values[g][:, lanes]

    def fill_centres():
        fill([y * (-2.0 * GAIN) for y in pick(0)], 0)

    fill([coeffs[g : g + 1] for g in range(3)], 8)
    gather_stages(table, (me, core, spot), table_sems, (nothing,) * 3, fill_centres)


def patch_tables(node_coords, node_disp, node_list, factor, coords, loads, blend, names):
    points = coords.shape[1]
    vmem = pl.BlockSpec(memory_space=VMEM)
    return pl.pallas_call(
        patch_kernel,
        out_shape=(
            jax.ShapeDtypeStruct((4, 4, 4, 2, 3, 16, LANES), f32),
            jax.ShapeDtypeStruct((FIELDS, 1, points), f32),
            jax.ShapeDtypeStruct((SLOTS, 1, points), jnp.int32),
        ),
        in_specs=[vmem] * 3 + [pl.BlockSpec(memory_space=pl.ANY)] + [vmem] * 4,
        out_specs=[vmem] * 3,
        scratch_shapes=[VMEM((4, 4, 4, 2, 3, 8, LANES), f32)]
        + factor_scratch()
        + stage_sems(True)
        + stage_sems(True),
        compiler_params=pltpu.CompilerParams(
            collective_id=0, has_side_effects=True, vmem_limit_bytes=60 * 2**20
        ),
    )(node_coords, node_disp, node_list, factor, coords, loads, blend, names)


def load_kernel(terms_hbm, ids, factor_hbm, out, spread, factor, high, low, marks, factor_sem, terms, terms_sem, *rest):
    patch_buffers, node_buffers = rest[:5], rest[5:10]
    patch_sems, node_sems = rest[10:16], rest[16:22]
    me, core, spot = place()
    load = pltpu.make_async_copy(factor_hbm, factor, factor_sem)
    fill = pltpu.make_async_copy(terms_hbm, terms, terms_sem)
    fill.start()
    load.start()
    barrier = greet(me, core, spot, True)
    mark_local(ids, marks)
    fill.wait()
    pl.semaphore_wait(barrier, PLANES)

    def ready_factor():
        load.wait()
        split_factor(factor, high, low)

    summed = sum_stages(terms, (me, core, spot), patch_buffers, patch_sems, ready_factor)
    rows = [jnp.concatenate([part[s : s + 1] for s in range(8)], axis=1) for part in summed]
    rows = jnp.concatenate(rows + [jnp.zeros((5, PN), f32)], axis=0)
    loads = apply_inverse(rows, high, low)
    where = at_owner(ids)
    parts = []
    for g in range(3):
        parts.extend(halves(jnp.where(where, loads[g : g + 1], 0.0)))
    found = lax.dot_general(
        jnp.concatenate(parts, axis=0),
        marks[...],
        (((1,), (1,)), ((), ())),
        preferred_element_type=f32,
    )
    flat = spread.reshape(PATCHES * 12, LANES)
    for g in range(3):
        base = 2 * g * PATCHES
        term = found[base : base + PATCHES] + found[base + PATCHES : base + 2 * PATCHES]
        for r in range(4):
            lanes = slice(r * LANES, (r + 1) * LANES)
            flat[pl.ds(4 * g + r, PATCHES, stride=12), :] = term[:, lanes]
    owned = sum_stages(spread, (me, core, spot), node_buffers, node_sems, nothing)
    for g in range(3):
        for r in range(4):
            out[pl.ds(g, 1), pl.ds(r * LANES, LANES)] = owned[g][r : r + 1]


def node_sums(terms, node_list, factor):
    vmem = pl.BlockSpec(memory_space=VMEM)
    hbm = pl.BlockSpec(memory_space=pl.ANY)
    return pl.pallas_call(
        load_kernel,
        out_shape=jax.ShapeDtypeStruct((3, NODE_DEV), f32),
        in_specs=[hbm, vmem, hbm],
        out_specs=vmem,
        scratch_shapes=[VMEM((4, 4, 4, 2, 3, 4, LANES), f32)]
        + factor_scratch()
        + [VMEM((4, 4, 4, 2, 3, 8, LANES), f32), pltpu.SemaphoreType.DMA]
        + sum_buffers(8)
        + sum_buffers(4)
        + stage_sems(False)
        + stage_sems(False),
        compiler_params=pltpu.CompilerParams(
            collective_id=1, has_side_effects=True, vmem_limit_bytes=60 * 2**20
        ),
    )(terms, node_list, factor)


FIELDS = 11
EARLY = 4


def fluid_kernel(*refs):
    patch, fields, table_hbm, disp, acc, work, table, held, table_sem, got = refs[:10]
    names, data = refs[10 : 10 + SLOTS], refs[10 + SLOTS :]
    fill = pltpu.make_async_copy(table_hbm, table, table_sem)
    fill.start()
    points = disp.shape[1]
    rows = [(patch.at[s], names[s]) for s in range(SLOTS)]
    rows += [(fields.at[j], data[j]) for j in range(FIELDS)]

    def scalars(k):
        first = EARLY * LANES
        where = (slice(None), pl.ds(first, points - first) if k else pl.ds(0, first))
        return [
            pltpu.make_async_copy(src.at[where], dst.at[where], got.at[k, j])
            for j, (src, dst) in enumerate(rows)
        ]

    for k in range(2):
        for copy in scalars(k):
            copy.start()
    def patch_step(p, _):
        y = [table[6 * p + 2 * c] for c in range(3)]
        total = (y[0] * y[0] + y[1] * y[1]) + y[2] * y[2]
        for c in range(3):
            work[p * 8 + c] = y[c]
            work[p * 8 + 4 + c] = table[6 * p + 2 * c + 1]
            acc[p * 3 + c] = jnp.zeros((8, LANES), f32)
        work[p * 8 + 3] = 1.0 + total * (1.0 / (4.0 * GAIN))
        return 0

    fill.wait()
    lax.fori_loop(0, PATCHES, patch_step, 0)

    for copy in scalars(0):
        copy.wait()

    def block_step(block, _):
        start = block * LANES

        @pl.when(block == EARLY)
        def _():
            for copy in scalars(1):
                copy.wait()

        for q in range(LANES):
            i = start + q
            x, y, z, square = data[0][0, i], data[1][0, i], data[2][0, i], data[6][0, i]
            ps = [names[s][0, i] for s in range(SLOTS)]
            term = []
            for s in range(SLOTS):
                p = ps[s] * 8
                near = (work[p] * x + work[p + 1] * y) + (work[p + 2] * z + (work[p + 3] + square))
                term.append(lax.rsqrt(near) * data[7 + s][0, i])
            old = [[acc[p * 3 + c] for c in range(3)] for p in ps]
            for c in range(3):
                dots = [work[ps[s] * 8 + 4 + c] * term[s] for s in range(SLOTS)]
                value = (dots[0] + dots[1]) + (dots[2] + dots[3])
                held[c, :, pl.ds(q, 1)] = jnp.sum(value, axis=1, keepdims=True)
            force = [data[3 + c][0, i] for c in range(3)]
            for s in range(SLOTS):
                for c in range(3):
                    acc[ps[s] * 3 + c] = old[s][c] + term[s] * force[c]
        for c in range(3):
            total = jnp.sum(held[c], axis=0, keepdims=True)
            disp[pl.ds(c, 1), pl.ds(pl.multiple_of(start, LANES), LANES)] = total * (1.0 / 32.0)
        return 0

    lax.fori_loop(0, points // LANES, block_step, 0)


def fluid(patch, fields, table):
    points = fields.shape[2]
    return pl.pallas_call(
        fluid_kernel,
        out_shape=(
            jax.ShapeDtypeStruct((3, points), f32),
            jax.ShapeDtypeStruct((PATCHES * 3, 8, LANES), f32),
        ),
        in_specs=[pl.BlockSpec(memory_space=pl.ANY)] * 3,
        out_specs=[pl.BlockSpec(memory_space=VMEM)] * 2,
        scratch_shapes=[
            VMEM((PATCHES * 8, 8, LANES), f32),
            VMEM((PATCHES * 6, 8, LANES), f32),
            VMEM((3, 8, LANES), f32),
            pltpu.SemaphoreType.DMA,
            pltpu.SemaphoreType.DMA((2, SLOTS + FIELDS)),
        ]
        + [pltpu.SMEM((1, points), jnp.int32)] * SLOTS
        + [pltpu.SMEM((1, points), f32)] * FIELDS,
    )(patch, fields, table)


def local(node_coords, node_disp, node_list, factor, fluid_coords, fluid_loads, fluid_patch, blend_raw):
    table, fields, names = patch_tables(
        node_coords,
        node_disp,
        node_list,
        factor[0],
        fluid_coords,
        fluid_loads,
        blend_raw.T,
        fluid_patch.T,
    )
    fluid_disp, terms = fluid(names, fields, table.reshape(PATCHES * 6, 8, LANES))
    node_loads = node_sums(terms.reshape(4, 4, 4, 2, 3, 8, LANES), node_list, factor[0])
    return fluid_disp, node_loads * (1.0 / 32.0)


def solution(mesh):
    placed = (
        P(None, "dev"),
        P(None, "dev"),
        P("dev", None),
        P("dev", None, None),
        P(None, "dev"),
        P(None, "dev"),
        P("dev", None),
        P("dev", None),
    )
    return jax.shard_map(
        local,
        mesh=mesh,
        in_specs=placed,
        out_specs=(P(None, "dev"), P(None, "dev")),
        check_vma=False,
    )
```
